768 devices in a mesh: lat: 48 (over z, y_hi, core), lon: 16 (over x, y_lo).
Axes of the slice: x: 4, y: 8 (y_hi: 2, y_lo: 4; y = y_hi * 4 + y_lo), z: 12, core: 2. Of those that a mesh axis runs over, the one named last changes fastest.
Arguments:
- fields: bfloat16 [192, 1440, 256], P('lat', 'lon'), may hold values from -6 to 6
- w_mix: bfloat16 [256, 1024], replicated, may hold values from -0.375 to 0.375
- filters: bfloat16 [4, 192, 3, 17], P(None, 'lat'), may hold values from -0.5 to 0.5
- reach: int32 [192], P('lat'), may hold values from 1 to 8, as said below
- w_up: bfloat16 [256, 512], replicated, may hold values from -0.375 to 0.375
- w_down: bfloat16 [512, 256], replicated, may hold values from -0.25 to 0.25
- cotangent: bfloat16 [192, 1440, 256], P('lat', 'lon'), may hold values from -6 to 6
Outputs:
- result: bfloat16 [192, 1440, 256], P('lat', 'lon')
- field_grad: bfloat16 [192, 1440, 256], P('lat', 'lon')
The draws below stay inside these ranges and needn't reach their ends.
Inputs may be any that keep to these rules, and one draw needn't show every extreme that they name: reach equals 8 at the two rows at each end of the grid.
All inputs are finite; a program needn't handle non-finite values.
Results may differ from the reference program's by a relative error of at most 0.0061.
Values may be sent and summed in bfloat16 or wider, within the bound.
A program may use at most 32 MiB of HBM per device.

```python
import jax
import jax.numpy as jnp
from jax import lax

CH = 256
HID = 512
KB = 4
LREACH = 8
NLAT = 192
NLON = 1440


def draw_reach(key, part):
    rows_index = jnp.arange(NLAT, dtype=jnp.int32)
    base = jax.random.randint(key, (NLAT,), 1, LREACH + 1, dtype=jnp.int32)
    polar = (rows_index < 2) | (rows_index >= NLAT - 2)
    return jnp.where(polar, LREACH, base).astype(jnp.int32)


def block_levels(own_key, shape, cuts, least, high):
    loudness = 1.0
    for dim, blocks in cuts:
        steps = jax.random.uniform(jax.random.fold_in(jax.random.fold_in(own_key, 6), dim), (blocks,), jnp.float32, least / len(cuts), high / len(cuts))
        loudness = loudness * jnp.repeat(jnp.exp(steps), shape[dim] // blocks).reshape((-1,) + (1,) * (len(shape) - 1 - dim))
    return loudness


def bell_draw(own_key, shape, width, bound, shards=(), held_as=jnp.bfloat16):
    gain = block_levels(own_key, shape, shards, -0.22, 0.18) if shards else 1.0
    entries = jax.random.normal(own_key, shape, jnp.float32) * width * gain
    return jnp.minimum(jnp.maximum(entries, -bound), bound).astype(held_as)


def setup_inputs(seed: int = 0) -> dict:
    seeds = jax.random.split(jax.random.key(seed), 8)
    fields = bell_draw(seeds[0], (NLAT, NLON, CH), 1.0, 6.0, ((0, 48), (1, 16)))
    w_mix = bell_draw(seeds[1], (CH, KB * CH), CH ** -0.5, 0.375)
    filters = bell_draw(seeds[2], (KB, NLAT, 3, 2 * LREACH + 1), 0.1, 0.5, ((1, 48),))
    reach = draw_reach(jax.random.fold_in(seeds[7], 71), 0)
    w_up = bell_draw(seeds[4], (CH, HID), CH ** -0.5, 0.375)
    w_down = bell_draw(seeds[5], (HID, CH), HID ** -0.5, 0.25)
    cotangent = bell_draw(seeds[6], (NLAT, NLON, CH), 1.0, 6.0, ((0, 48), (1, 16)))
    return {"fields": fields, "w_mix": w_mix, "filters": filters, "reach": reach, "w_up": w_up, "w_down": w_down, "cotangent": cotangent}


def gelu_value(pre):
    return 0.5 * pre * (1.0 + jax.scipy.special.erf(pre * 0.7071067811865476))


def gelu_slope(pre):
    return 0.5 * (1.0 + jax.scipy.special.erf(pre * 0.7071067811865476)) + pre * jnp.exp(-0.5 * pre * pre) * 0.3989422804014327


def masked_filters(filters, reach):
    offsets = jnp.arange(2 * LREACH + 1, dtype=jnp.int32) - LREACH
    keep = (jnp.abs(offsets)[None, :] <= reach[:, None]).astype(filters.dtype)
    return filters * keep[None, :, None, :]


def contract_last(left, right):
    return lax.dot_general(left, right, (((1,), (1,)), ((), ())), preferred_element_type=jnp.float32)


def reference(fields, w_mix, filters, reach, w_up, w_down, cotangent):
    span_taps = 2 * LREACH + 1
    masked = masked_filters(filters, reach)
    mixed = jnp.dot(fields.reshape(-1, CH), w_mix, preferred_element_type=jnp.float32).astype(jnp.bfloat16)
    mixed = mixed.reshape(NLAT, NLON, KB, CH)
    padded = jnp.pad(mixed, ((1, 1), (0, 0), (0, 0), (0, 0)))

    def forward_row(index):
        block = lax.dynamic_slice_in_dim(padded, index, 3, 0).astype(jnp.float32)
        weights = lax.dynamic_slice_in_dim(masked, index, 1, 1)[:, 0].astype(jnp.float32)
        total = jnp.zeros((NLON, CH), jnp.float32)
        for tap in range(span_taps):
            moved = jnp.roll(block, LREACH - tap, axis=1)
            total = total + jnp.einsum("ka,ajkc->jc", weights[:, :, tap], moved, precision=lax.Precision.HIGHEST)
        return total

    spatial = lax.map(forward_row, jnp.arange(NLAT, dtype=jnp.int32))
    hidden = (fields.astype(jnp.float32) + spatial).astype(jnp.bfloat16)
    flat_hidden = hidden.reshape(-1, CH)
    pre = jnp.dot(flat_hidden, w_up, preferred_element_type=jnp.float32)
    active = gelu_value(pre).astype(jnp.bfloat16)
    result = (flat_hidden.astype(jnp.float32) + jnp.dot(active, w_down, preferred_element_type=jnp.float32)).astype(jnp.bfloat16)
    upstream = cotangent.reshape(-1, CH)
    grad_active = (contract_last(upstream, w_down) * gelu_slope(pre)).astype(jnp.bfloat16)
    grad_hidden = (upstream.astype(jnp.float32) + contract_last(grad_active, w_up)).astype(jnp.bfloat16)
    grad_pad = jnp.pad(grad_hidden.reshape(NLAT, NLON, CH), ((1, 1), (0, 0), (0, 0)))
    masked_pad = jnp.pad(masked, ((0, 0), (1, 1), (0, 0), (0, 0)))

    def backward_row(index):
        block = lax.dynamic_slice_in_dim(grad_pad, index, 3, 0).astype(jnp.float32)
        near = lax.dynamic_slice_in_dim(masked_pad, index, 3, 1).astype(jnp.float32)
        weights = jnp.stack([near[:, step, 2 - step] for step in range(3)], axis=1)
        total = jnp.zeros((NLON, KB, CH), jnp.float32)
        for tap in range(span_taps):
            moved = jnp.roll(block, tap - LREACH, axis=1)
            total = total + jnp.einsum("kt,tjc->jkc", weights[:, :, tap], moved, precision=lax.Precision.HIGHEST)
        return total.astype(jnp.bfloat16).reshape(NLON, KB * CH)

    grad_mixed = lax.map(backward_row, jnp.arange(NLAT, dtype=jnp.int32))
    field_grad = grad_hidden.astype(jnp.float32) + contract_last(grad_mixed.reshape(-1, KB * CH), w_mix)
    field_grad = field_grad.astype(jnp.bfloat16).reshape(NLAT, NLON, CH)
    return result.reshape(NLAT, NLON, CH), field_grad
```

```python
import functools

import jax
import jax.numpy as jnp
from jax import lax
from jax.experimental import pallas as pl
from jax.experimental.pallas import tpu as pltpu
from jax.sharding import PartitionSpec as P

KB = 4
REACH = 8
TAPS = 2 * REACH + 1
WIDE = 2 * REACH
CH = 256
HID = 512
ROWS = 4
RING = 128
CELLS = 112
OUTC = 96
MESH = pl.DeviceIdType.MESH
F32 = jnp.float32
BF16 = jnp.bfloat16


def dot(left, right):
    return jnp.dot(left, right, preferred_element_type=F32)


def dot_last(left, right):
    return lax.dot_general(left, right, (((1,), (1,)), ((), ())), preferred_element_type=F32)


def circulant(taps, count, start):
    spread = jnp.broadcast_to(taps, (count, RING))
    return pltpu.roll(spread, (start - REACH) % RING, 1, stride=1, stride_axis=0)


def tap_row(row, tap, basis):
    return ((2 - tap) if row in (-1, ROWS) else tap) * KB + basis


def place():
    lat, lon = lax.axis_index("lat"), lax.axis_index("lon")
    lats, lons = lax.axis_size("lat"), lax.axis_size("lon")
    odd = lax.rem(lat, 2)
    near = jnp.where(odd == 1, lat - 1, lat + 1)
    far = jnp.where(odd == 1, lat + 1, lat - 1)
    has_far = jnp.logical_and(far >= 0, far < lats)
    west = lax.rem(lon + lons - 1, lons)
    east = lax.rem(lon + 1, lons)
    return lat, lon, odd, near, far, has_far, west, east


def owned(odd, row):
    return jnp.where(odd == 1, row, ROWS - 1 - row)


def forward_kernel(
    width,
    fields_hbm, cot_hbm, w_mix_hbm, w_up_hbm, w_down_hbm, filters_ref, reach_ref,
    result_ref, grads_ref, back_ref,
    own, edge, cot_w, cot_e, taps_own, near_in, far_in, taps_near, taps_far,
    w_in, e_in, cw_in, ce_in, nw_in, ne_in, ncw_in, nce_in, fw_in, fe_in, fcw_in, fce_in,
    cells, cots, taps, taps_rev, fwd, w_mix, w_up, w_down,
    load_sem, send_sem, recv_sem,
):
    lat, lon, odd, near, far, has_far, west, east = place()

    barrier = pltpu.get_barrier_semaphore()

    def greet(target):
        pl.semaphore_signal(barrier, inc=1, device_id=target, device_id_type=MESH)

    for target in ((lat, west), (lat, east), (near, lon), (near, west), (near, east)):
        greet(target)

    @pl.when(has_far)
    def _():
        for target in ((far, lon), (far, west), (far, east)):
            greet(target)

    loads = []
    for row in range(ROWS):
        loads.append((fields_hbm.at[owned(odd, row)], own.at[1 + row]))
        loads.append((cot_hbm.at[owned(odd, row)], own.at[(0, 6, 7, 5)[row]]))
    loads += [(w_mix_hbm, w_mix), (w_up_hbm, w_up), (w_down_hbm, w_down)]
    loads = [pltpu.make_async_copy(s, d, load_sem.at[i]) for i, (s, d) in enumerate(loads)]
    for load in loads:
        load.start()

    taps[...] = jnp.zeros_like(taps)
    lane = lax.broadcasted_iota(jnp.int32, (1, TAPS), 1) - REACH
    for row in range(ROWS):
        keep = jnp.abs(lane) <= reach_ref[owned(odd, row)]
        for basis in range(KB):
            block = filters_ref[basis, owned(odd, row)].astype(F32)
            for tap in range(3):
                value = jnp.where(odd == 1, block[tap : tap + 1], block[2 - tap : 3 - tap])
                taps[1 + row, pl.ds(tap * KB + basis, 1), 0:TAPS] = jnp.where(keep, value, 0.0)
    taps_own[0] = taps[1].astype(BF16)
    taps_own[1] = taps[ROWS].astype(BF16)

    for load in loads[: 2 * ROWS]:
        load.wait()
    edge[...] = own[1:5, width - WIDE : width]
    for row, slot in enumerate((0, 6, 7, 5)):
        cot_w[row] = own[slot, 0:REACH]
        cot_e[row] = own[slot, width - REACH : width]

    pl.semaphore_wait(barrier, 5 + jnp.where(has_far, 3, 0))

    def remote(index, source, target, device):
        return pltpu.make_async_remote_copy(
            src_ref=source, dst_ref=target, send_sem=send_sem.at[index],
            recv_sem=recv_sem.at[index], device_id=device, device_id_type=MESH,
        )

    head = pl.ds(0, WIDE)
    far_sends = [
        remote(0, own.at[pl.ds(3, 3)], far_in, (far, lon)),
        remote(1, taps_own.at[1], taps_far, (far, lon)),
        remote(2, own.at[pl.ds(3, 2), head], fe_in, (far, west)),
        remote(3, cot_w.at[3], fce_in, (far, west)),
        remote(4, edge.at[pl.ds(2, 2)], fw_in, (far, east)),
        remote(5, cot_e.at[3], fcw_in, (far, east)),
    ]
    lon_sends = [
        remote(6, own.at[pl.ds(1, 4), head], e_in, (lat, west)),
        remote(7, cot_w, ce_in, (lat, west)),
        remote(8, edge, w_in, (lat, east)),
        remote(9, cot_e, cw_in, (lat, east)),
    ]
    near_sends = [
        remote(10, own.at[pl.ds(0, 3)], near_in, (near, lon)),
        remote(11, taps_own.at[0], taps_near, (near, lon)),
        remote(12, own.at[pl.ds(1, 2), head], ne_in, (near, west)),
        remote(13, cot_w.at[0], nce_in, (near, west)),
        remote(14, edge.at[pl.ds(0, 2)], nw_in, (near, east)),
        remote(15, cot_e.at[0], ncw_in, (near, east)),
    ]

    @pl.when(has_far)
    def _():
        for copy in far_sends:
            copy.start()

    for copy in lon_sends + near_sends:
        copy.start()

    @pl.when(jnp.logical_not(has_far))
    def _():
        for ref in (far_in, taps_far, fe_in, fce_in, fw_in, fcw_in):
            ref[...] = jnp.zeros_like(ref)

    first = lax.broadcasted_iota(jnp.int32, (RING, RING), 0)
    second = lax.broadcasted_iota(jnp.int32, (RING, RING), 1)
    flip = (first + second == 2 * REACH).astype(BF16)

    def reverse(row):
        taps_rev[row + 1] = dot(taps[row + 1].astype(BF16), flip)

    def forward_matrix(row):
        for tap in range(3):
            for basis in range(KB):
                line = taps[row + 1, pl.ds(tap_row(row, tap, basis), 1), :]
                block = jnp.concatenate(
                    [circulant(line, 104, 0), circulant(line, REACH, RING - REACH)], axis=0
                )
                fwd[row + 1, basis * CELLS : (basis + 1) * CELLS, tap * RING : (tap + 1) * RING] = (
                    block.astype(BF16)
                )

    def backward_blocks(source):
        for out in range(max(0, source - 1), min(ROWS, source + 2)):
            tap, slot = out - source + 1, source - out + 1
            for basis in range(KB):
                line = taps_rev[source + 1, pl.ds(tap_row(source, tap, basis), 1), :]
                back_ref[out, basis * OUTC : (basis + 1) * OUTC, slot * RING : (slot + 1) * RING] = (
                    circulant(line, OUTC, 0).astype(BF16)
                )

    for row in range(ROWS):
        reverse(row)
        forward_matrix(row)
        backward_blocks(row)

    for load in loads[2 * ROWS :]:
        load.wait()

    def fill_cells(row, middle, west_part, east_part):
        cells[row + 2, 0:width] = middle
        cells[row + 2, width : width + WIDE] = east_part
        cells[row + 2, width + WIDE : RING - WIDE] = jnp.zeros(
            (RING - 2 * WIDE - width, CH), BF16
        )
        cells[row + 2, RING - WIDE : RING] = west_part

    def fill_cots(row, middle, west_part, east_part):
        cots[row + 1, 0:width] = middle
        cots[row + 1, width : width + REACH] = east_part
        cots[row + 1, width + REACH : 104] = jnp.zeros((104 - REACH - width, CH), BF16)
        cots[row + 1, 104:CELLS] = west_part

    def advance(rows):
        count = len(rows)
        convs = []
        for row in rows:
            source = cells[row + 1 : row + 4].reshape(3 * RING, CH)
            convs.append(dot(fwd[row + 1], source).astype(BF16))
        spatial = jnp.zeros((count * CELLS, CH), F32)
        for basis in range(KB):
            part = jnp.concatenate(
                [c[basis * CELLS : (basis + 1) * CELLS] for c in convs], axis=0
            )
            spatial = spatial + dot(part, w_mix[:, basis * CH : (basis + 1) * CH])
        centre = jnp.concatenate(
            [p for row in rows for p in (cells[row + 2, 0:104].astype(F32), cells[row + 2, 120:128].astype(F32))],
            axis=0,
        )
        hidden = (centre + spatial).astype(BF16)
        pre = dot(hidden, w_up[...])
        half = 0.5 * (1.0 + lax.erf(pre * 0.7071067811865476))
        slope = half + pre * jnp.exp(-0.5 * pre * pre) * 0.3989422804014327
        upstream = jnp.concatenate([cots[row + 1] for row in rows], axis=0)
        grad_active = (dot_last(upstream, w_down[...]) * slope).astype(BF16)
        grad = (upstream.astype(F32) + dot_last(grad_active, w_up[...])).astype(BF16)
        active = (half * pre).astype(BF16)
        for n, row in enumerate(rows):
            base = n * CELLS
            grads_ref[row + 1, 0:104] = grad[base : base + 104]
            grads_ref[row + 1, 104:120] = jnp.zeros((WIDE, CH), BF16)
            grads_ref[row + 1, 120:128] = grad[base + 104 : base + CELLS]
            if 0 <= row < ROWS:
                result = hidden[base : base + OUTC].astype(F32) + dot(
                    active[base : base + OUTC], w_down[...]
                )
                result_ref[row] = result[:width].astype(BF16)

    for copy in lon_sends:
        copy.wait_recv()
    for row in range(ROWS):
        fill_cells(row, own[1 + row], w_in[row], e_in[row])
        fill_cots(row, own[(0, 6, 7, 5)[row]], cw_in[row], ce_in[row])
    advance((1, 2))

    for copy in near_sends:
        copy.wait_recv()
    taps[0] = taps_near[...].astype(F32)
    reverse(-1)
    forward_matrix(-1)
    backward_blocks(-1)
    fill_cells(-1, near_in[1], nw_in[0], ne_in[0])
    fill_cells(-2, near_in[2], nw_in[1], ne_in[1])
    fill_cots(-1, near_in[0], ncw_in[...], nce_in[...])
    advance((0, -1))

    @pl.when(has_far)
    def _():
        for copy in far_sends:
            copy.wait_recv()

    taps[ROWS + 1] = taps_far[...].astype(F32)
    reverse(ROWS)
    forward_matrix(ROWS)
    backward_blocks(ROWS)
    fill_cells(ROWS, far_in[1], fw_in[1], fe_in[1])
    fill_cells(ROWS + 1, far_in[0], fw_in[0], fe_in[0])
    fill_cots(ROWS, far_in[2], fcw_in[...], fce_in[...])
    advance((3, 4))

    for copy in lon_sends + near_sends:
        copy.wait_send()

    @pl.when(has_far)
    def _():
        for copy in far_sends:
            copy.wait_send()


def backward_kernel(width, result_in, grads_ref, back_ref, w_mix_hbm, result_hbm, grad_hbm, out, w_mix, sems):
    odd = lax.rem(lax.axis_index("lat"), 2)
    weights = pltpu.make_async_copy(w_mix_hbm, w_mix, sems.at[8])
    weights.start()
    copies = [
        pltpu.make_async_copy(result_in.at[row], result_hbm.at[owned(odd, row)], sems.at[row])
        for row in range(ROWS)
    ]
    for copy in copies:
        copy.start()
    weights.wait()
    for rows in ((0, 1), (2, 3)):
        convs = []
        for row in rows:
            source = grads_ref[row : row + 3].reshape(3 * RING, CH)
            convs.append(dot(back_ref[row], source).astype(BF16))
        total = jnp.concatenate([grads_ref[row + 1, 0:OUTC].astype(F32) for row in rows], axis=0)
        for basis in range(KB):
            part = jnp.concatenate([c[basis * OUTC : (basis + 1) * OUTC] for c in convs], axis=0)
            total = total + dot_last(part, w_mix[:, basis * CH : (basis + 1) * CH])
        for n, row in enumerate(rows):
            out[row] = total[n * OUTC : n * OUTC + width].astype(BF16)
            copy = pltpu.make_async_copy(
                out.at[row], grad_hbm.at[owned(odd, row)], sems.at[ROWS + row]
            )
            copy.start()
            copies.append(copy)
    for copy in copies:
        copy.wait()


def on_device(fields, w_mix, filters, reach, w_up, w_down, cotangent):
    rows, width, chans = fields.shape
    hbm = pl.BlockSpec(memory_space=pltpu.HBM)
    vmem = pl.BlockSpec(memory_space=pltpu.VMEM)
    smem = pl.BlockSpec(memory_space=pltpu.SMEM)

    def held(*shape, kind=BF16):
        return pltpu.VMEM(shape, kind)

    result, grads, back = pl.pallas_call(
        functools.partial(forward_kernel, width),
        name="halo_forward",
        out_shape=(
            jax.ShapeDtypeStruct((rows, width, chans), BF16),
            jax.ShapeDtypeStruct((rows + 2, RING, chans), BF16),
            jax.ShapeDtypeStruct((rows, KB * OUTC, 3 * RING), BF16),
        ),
        in_specs=[hbm] * 5 + [vmem, smem],
        out_specs=(vmem, vmem, vmem),
        scratch_shapes=[
            held(8, width, chans),
            held(rows, WIDE, chans),
            held(rows, REACH, chans),
            held(rows, REACH, chans),
            held(2, 16, RING),
            held(3, width, chans),
            held(3, width, chans),
            held(16, RING),
            held(16, RING),
            held(rows, WIDE, chans),
            held(rows, WIDE, chans),
            held(rows, REACH, chans),
            held(rows, REACH, chans),
            held(2, WIDE, chans),
            held(2, WIDE, chans),
            held(REACH, chans),
            held(REACH, chans),
            held(2, WIDE, chans),
            held(2, WIDE, chans),
            held(REACH, chans),
            held(REACH, chans),
            held(rows + 4, RING, chans),
            held(rows + 2, CELLS, chans),
            held(rows + 2, 16, RING, kind=F32),
            held(rows + 2, 16, RING, kind=F32),
            held(rows + 2, KB * CELLS, 3 * RING),
            held(chans, KB * chans),
            held(chans, HID),
            held(HID, chans),
            pltpu.SemaphoreType.DMA((11,)),
            pltpu.SemaphoreType.DMA((16,)),
            pltpu.SemaphoreType.DMA((16,)),
        ],
        compiler_params=pltpu.CompilerParams(
            collective_id=0, has_side_effects=True, vmem_limit_bytes=24 << 20
        ),
    )(fields, cotangent, w_mix, w_up, w_down, filters, reach)
    return pl.pallas_call(
        functools.partial(backward_kernel, width),
        name="transposed_mix",
        out_shape=(
            jax.ShapeDtypeStruct((rows, width, chans), BF16),
            jax.ShapeDtypeStruct((rows, width, chans), BF16),
        ),
        in_specs=[vmem, vmem, vmem, hbm],
        out_specs=(hbm, hbm),
        scratch_shapes=[
            held(rows, width, chans),
            held(chans, KB * chans),
            pltpu.SemaphoreType.DMA((9,)),
        ],
        compiler_params=pltpu.CompilerParams(vmem_limit_bytes=16 << 20),
    )(result, grads, back, w_mix)


def solution(mesh):
    return jax.shard_map(
        on_device,
        mesh=mesh,
        in_specs=(
            P("lat", "lon", None),
            P(),
            P(None, "lat", None, None),
            P("lat"),
            P(),
            P(),
            P("lat", "lon", None),
        ),
        out_specs=(P("lat", "lon", None), P("lat", "lon", None)),
        check_vma=False,
    )
```

```python
import functools

import jax
import jax.numpy as jnp
from jax import lax
from jax.experimental import pallas as pl
from jax.experimental.pallas import tpu as pltpu
from jax.sharding import PartitionSpec as P

KB = 4
REACH = 8
TAPS = 2 * REACH + 1
WIDE = 2 * REACH
CH = 256
HID = 512
ROWS = 4
LANES = 128
RING = 128
CELLS = 112
OUTC = 96
MESH = pl.DeviceIdType.MESH
F32 = jnp.float32
BF16 = jnp.bfloat16


def dot(left, right):
    return jnp.dot(left, right, preferred_element_type=F32)


def dot_last(left, right):
    return lax.dot_general(left, right, (((1,), (1,)), ((), ())), preferred_element_type=F32)


def circulant(taps, count, start):
    spread = jnp.broadcast_to(taps, (count, RING))
    return pltpu.roll(spread, (start - REACH) % RING, 1, stride=1, stride_axis=0)


def packed(grid):
    rows, width, chans = grid.shape
    tiles = grid.transpose(1, 0, 2).reshape(width, rows, chans // LANES, LANES)
    return tiles.transpose(0, 2, 1, 3).reshape(width * rows * chans // LANES, LANES)


def unpacked(tiles, rows, width, chans):
    grid = tiles.reshape(width, chans // LANES, rows, LANES).transpose(0, 2, 1, 3)
    return grid.reshape(width, rows, chans).transpose(1, 0, 2)


def read_row(tiles, row, width):
    return jnp.concatenate(
        [tiles[pl.ds(half * ROWS + row, width, stride=2 * ROWS), :] for half in range(2)], axis=1
    )


def write_row(tiles, row, width, value):
    for half in range(2):
        tiles[pl.ds(half * ROWS + row, width, stride=2 * ROWS), :] = value[
            :, half * LANES : (half + 1) * LANES
        ]


def place():
    lat, lon = lax.axis_index("lat"), lax.axis_index("lon")
    lats, lons = lax.axis_size("lat"), lax.axis_size("lon")
    odd = lax.rem(lat, 2)
    near = jnp.where(odd == 1, lat - 1, lat + 1)
    far = jnp.where(odd == 1, lat + 1, lat - 1)
    has_far = jnp.logical_and(far >= 0, far < lats)
    west = lax.rem(lon + lons - 1, lons)
    east = lax.rem(lon + 1, lons)
    return lat, lon, odd, near, far, has_far, west, east


def owned(odd, row):
    return jnp.where(odd == 1, row, ROWS - 1 - row)


def forward_kernel(
    width,
    fields_hbm, cot_hbm, w_mix_hbm, w_up_hbm, w_down_hbm, filters_hbm, reach_hbm,
    result_ref, grads_ref, back_ref, w_mix, done_ref,
    raw, raw_cot, wide, filters_ref, filters_wide, reach_ref,
    own, edge, cot_w, cot_e, taps_own, near_in, far_in, taps_near, taps_far,
    w_in, e_in, cw_in, ce_in, nw_in, ne_in, ncw_in, nce_in, fw_in, fe_in, fcw_in, fce_in,
    cells, cots, taps, taps_rev, fwd, partial_ref, w_up, w_down,
    load_sem, send_sem, recv_sem,
):
    lat, lon, odd, near, far, has_far, west, east = place()

    barrier = pltpu.get_barrier_semaphore()

    def greet(target):
        pl.semaphore_signal(barrier, inc=1, device_id=target, device_id_type=MESH)

    last = jnp.logical_and(lat == 0, lon == 0)
    close = ((lat, west), (lat, east), (near, lon), (near, west), (near, east))
    to_last = [jnp.logical_and(a == 0, o == 0) for a, o in close]
    n_last = sum(flag.astype(jnp.int32) for flag in to_last)
    for target, flag in zip(close, to_last):
        pl.when(jnp.logical_not(jnp.logical_or(last, flag)))(functools.partial(greet, target))

    @pl.when(has_far)
    def _():
        for target in ((far, lon), (far, west), (far, east)):
            greet(target)

    loads = [
        (fields_hbm, raw), (cot_hbm, raw_cot), (filters_hbm, filters_ref), (reach_hbm, reach_ref),
        (w_mix_hbm, w_mix), (w_up_hbm, w_up), (w_down_hbm, w_down),
    ]
    loads = [pltpu.make_async_copy(s, d, load_sem.at[i]) for i, (s, d) in enumerate(loads)]
    for load in loads:
        load.start()

    for load, source, slots in ((loads[0], raw, (1, 2, 3, 4)), (loads[1], raw_cot, (0, 6, 7, 5))):
        load.wait()
        wide[...] = source[...].astype(F32)
        for row in range(ROWS):
            own[slots[row]] = read_row(wide, owned(odd, row), width).astype(BF16)

    loads[2].wait()
    loads[3].wait()
    taps[...] = jnp.zeros_like(taps)
    filters_wide[...] = filters_ref[...].astype(F32)
    lane = lax.broadcasted_iota(jnp.int32, (1, TAPS), 1) - REACH
    for row in range(ROWS):
        keep = jnp.abs(lane) <= reach_ref[owned(odd, row)]
        lines = filters_wide[pl.ds(owned(odd, row), 3 * KB, stride=ROWS), :]
        taps[1 + row, 0 : 3 * KB, 0:TAPS] = jnp.where(keep, lines, 0.0)
    taps_own[0] = taps[1].astype(BF16)
    taps_own[1] = taps[ROWS].astype(BF16)

    edge[...] = own[1:5, width - WIDE : width]
    for row, slot in enumerate((0, 6, 7, 5)):
        cot_w[row] = own[slot, 0:REACH]
        cot_e[row] = own[slot, width - REACH : width]

    pl.semaphore_wait(barrier, 5 - n_last + jnp.where(has_far, 3, 0))
    for target, flag in zip(close, to_last):
        pl.when(jnp.logical_or(last, flag))(functools.partial(greet, target))

    def remote(index, source, target, device):
        return pltpu.make_async_remote_copy(
            src_ref=source, dst_ref=target, send_sem=send_sem.at[index],
            recv_sem=recv_sem.at[index], device_id=device, device_id_type=MESH,
        )

    head = pl.ds(0, WIDE)
    far_sends = [
        remote(0, taps_own.at[1], taps_far, (far, lon)),
        remote(1, own.at[pl.ds(3, 3)], far_in, (far, lon)),
        remote(2, own.at[pl.ds(3, 2), head], fe_in, (far, west)),
        remote(3, cot_w.at[3], fce_in, (far, west)),
        remote(4, edge.at[pl.ds(2, 2)], fw_in, (far, east)),
        remote(5, cot_e.at[3], fcw_in, (far, east)),
    ]
    west_sends = [
        remote(6, own.at[pl.ds(1, 4), head], e_in, close[0]),
        remote(7, cot_w, ce_in, close[0]),
    ]
    east_sends = [
        remote(8, edge, w_in, close[1]),
        remote(9, cot_e, cw_in, close[1]),
    ]
    mate_sends = [
        remote(10, taps_own.at[0], taps_near, close[2]),
        remote(11, own.at[pl.ds(0, 3)], near_in, close[2]),
    ]
    mate_west_sends = [
        remote(12, own.at[pl.ds(1, 2), head], ne_in, close[3]),
        remote(13, cot_w.at[0], nce_in, close[3]),
    ]
    mate_east_sends = [
        remote(14, edge.at[pl.ds(0, 2)], nw_in, close[4]),
        remote(15, cot_e.at[0], ncw_in, close[4]),
    ]
    groups = (west_sends, east_sends, mate_sends, mate_west_sends, mate_east_sends)
    lon_sends = west_sends + east_sends
    near_sends = mate_sends + mate_west_sends + mate_east_sends

    def start(copies):
        for copy in copies:
            copy.start()

    pl.when(has_far)(functools.partial(start, far_sends[:1] + far_sends[2:]))
    for copies, flag in zip(groups, to_last):
        pl.when(jnp.logical_not(flag))(functools.partial(start, copies))
    pl.when(has_far)(functools.partial(start, far_sends[1:2]))

    @pl.when(n_last > 0)
    def _():
        pl.semaphore_wait(barrier, n_last)

    for copies, flag in zip(groups, to_last):
        pl.when(flag)(functools.partial(start, copies))

    @pl.when(jnp.logical_not(has_far))
    def _():
        for ref in (far_in, taps_far, fe_in, fce_in, fw_in, fcw_in):
            ref[...] = jnp.zeros_like(ref)

    first = lax.broadcasted_iota(jnp.int32, (RING, RING), 0)
    second = lax.broadcasted_iota(jnp.int32, (RING, RING), 1)
    flip = (first + second == 2 * REACH).astype(BF16)

    def tap_line(tap, basis):
        return basis * 3 + jnp.where(odd == 1, tap, 2 - tap)

    def reverse(row):
        taps_rev[row + 1] = dot(taps[row + 1].astype(BF16), flip)

    def forward_matrix(row):
        for tap in range(3):
            for basis in range(KB):
                line = taps[row + 1, pl.ds(tap_line(tap, basis), 1), :]
                block = jnp.concatenate(
                    [circulant(line, 104, 0), circulant(line, REACH, RING - REACH)], axis=0
                )
                fwd[row + 1, basis * CELLS : (basis + 1) * CELLS, tap * RING : (tap + 1) * RING] = (
                    block.astype(BF16)
                )

    def backward_blocks(source):
        for out in range(max(0, source - 1), min(ROWS, source + 2)):
            tap, slot = out - source + 1, source - out + 1
            for basis in range(KB):
                line = taps_rev[source + 1, pl.ds(tap_line(tap, basis), 1), :]
                back_ref[out, basis * OUTC : (basis + 1) * OUTC, slot * RING : (slot + 1) * RING] = (
                    circulant(line, OUTC, 0).astype(BF16)
                )

    for row in range(ROWS):
        reverse(row)
        forward_matrix(row)
        backward_blocks(row)

    for load in loads[4:]:
        load.wait()

    def fill_cells(row, middle, west_part, east_part):
        cells[row + 2, 0:width] = middle
        cells[row + 2, width : width + WIDE] = east_part
        cells[row + 2, width + WIDE : RING - WIDE] = jnp.zeros(
            (RING - 2 * WIDE - width, CH), BF16
        )
        cells[row + 2, RING - WIDE : RING] = west_part

    def fill_cots(row, middle, west_part, east_part):
        cots[row + 1, 0:width] = middle
        cots[row + 1, width : width + REACH] = east_part
        cots[row + 1, width + REACH : 104] = jnp.zeros((104 - REACH - width, CH), BF16)
        cots[row + 1, 104:CELLS] = west_part

    def conv_part(row, begin, end):
        source = cells[row + 1 + begin : row + 1 + end].reshape((end - begin) * RING, CH)
        return dot(fwd[row + 1, :, begin * RING : end * RING], source)

    def advance(rows, ready=None):
        count = len(rows)
        convs = []
        for n, row in enumerate(rows):
            if ready is None:
                conv = conv_part(row, 0, 3)
            else:
                conv = partial_ref[n] + conv_part(row, ready[n], 3)
            convs.append(conv.astype(BF16))
        spatial = jnp.zeros((count * CELLS, CH), F32)
        for basis in range(KB):
            part = jnp.concatenate(
                [c[basis * CELLS : (basis + 1) * CELLS] for c in convs], axis=0
            )
            spatial = spatial + dot(part, w_mix[:, basis * CH : (basis + 1) * CH])
        centre = jnp.concatenate(
            [p for row in rows for p in (cells[row + 2, 0:104].astype(F32), cells[row + 2, 120:128].astype(F32))],
            axis=0,
        )
        hidden = (centre + spatial).astype(BF16)
        pre = dot(hidden, w_up[...])
        half = 0.5 * (1.0 + lax.erf(pre * 0.7071067811865476))
        slope = half + pre * jnp.exp(-0.5 * pre * pre) * 0.3989422804014327
        upstream = jnp.concatenate([cots[row + 1] for row in rows], axis=0)
        grad_active = (dot_last(upstream, w_down[...]) * slope).astype(BF16)
        grad = (upstream.astype(F32) + dot_last(grad_active, w_up[...])).astype(BF16)
        active = (half * pre).astype(BF16)
        for n, row in enumerate(rows):
            base = n * CELLS
            grads_ref[row + 1, 0:104] = grad[base : base + 104]
            grads_ref[row + 1, 104:120] = jnp.zeros((WIDE, CH), BF16)
            grads_ref[row + 1, 120:128] = grad[base + 104 : base + CELLS]
            if 0 <= row < ROWS:
                result = hidden[base : base + OUTC].astype(F32) + dot(
                    active[base : base + OUTC], w_down[...]
                )
                write_row(wide, owned(odd, row), width, result[:width])

    def finish(rows):
        return retreat(rows, grads_ref, back_ref, w_mix)

    for copy in lon_sends:
        copy.wait_recv()
    for row in range(ROWS):
        fill_cells(row, own[1 + row], w_in[row], e_in[row])
        fill_cots(row, own[(0, 6, 7, 5)[row]], cw_in[row], ce_in[row])
    advance((1, 2))

    mate_sends[0].wait_recv()
    taps[0] = taps_near[...].astype(F32)
    reverse(-1)
    forward_matrix(-1)
    backward_blocks(-1)
    for copy in near_sends[1:]:
        copy.wait_recv()
    fill_cells(-1, near_in[1], nw_in[0], ne_in[0])
    fill_cells(-2, near_in[2], nw_in[1], ne_in[1])
    fill_cots(-1, near_in[0], ncw_in[...], nce_in[...])
    advance((0, -1))
    done_ref[...] = finish((0, 1))

    pl.when(has_far)(far_sends[0].wait_recv)
    taps[ROWS + 1] = taps_far[...].astype(F32)
    reverse(ROWS)
    forward_matrix(ROWS)
    backward_blocks(ROWS)
    partial_ref[0] = conv_part(ROWS - 1, 0, 2)
    partial_ref[1] = conv_part(ROWS, 0, 1)

    @pl.when(has_far)
    def _():
        for copy in far_sends[1:]:
            copy.wait_recv()

    fill_cells(ROWS, far_in[1], fw_in[1], fe_in[1])
    fill_cells(ROWS + 1, far_in[0], fw_in[0], fe_in[0])
    fill_cots(ROWS, far_in[2], fcw_in[...], fce_in[...])
    advance((ROWS - 1, ROWS), ready=(2, 1))
    result_ref[...] = wide[...].astype(BF16)

    for copies in groups:
        for copy in copies:
            copy.wait_send()

    @pl.when(has_far)
    def _():
        for copy in far_sends:
            copy.wait_send()


def retreat(rows, grads_ref, back_ref, w_mix):
    convs = []
    for row in rows:
        source = grads_ref[row : row + 3].reshape(3 * RING, CH)
        convs.append(dot(back_ref[row], source).astype(BF16))
    total = jnp.concatenate([grads_ref[row + 1, 0:OUTC].astype(F32) for row in rows], axis=0)
    for basis in range(KB):
        part = jnp.concatenate([c[basis * OUTC : (basis + 1) * OUTC] for c in convs], axis=0)
        total = total + dot_last(part, w_mix[:, basis * CH : (basis + 1) * CH])
    return total


def backward_kernel(
    width, packed_result, grads_ref, back_ref, w_mix, done_ref, result_hbm, grad_hbm, wide, out, sems
):
    odd = lax.rem(lax.axis_index("lat"), 2)
    store_result = pltpu.make_async_copy(packed_result, result_hbm, sems.at[0])
    store_result.start()
    total = retreat((2, 3), grads_ref, back_ref, w_mix)
    for row in (0, 1):
        write_row(wide, owned(odd, row), width, done_ref[row * OUTC : row * OUTC + width])
        write_row(wide, owned(odd, 2 + row), width, total[row * OUTC : row * OUTC + width])
    out[...] = wide[...].astype(BF16)
    store_grad = pltpu.make_async_copy(out, grad_hbm, sems.at[1])
    store_grad.start()
    store_result.wait()
    store_grad.wait()


def on_device(fields, w_mix, filters, reach, w_up, w_down, cotangent):
    rows, width, chans = fields.shape
    hbm = pl.BlockSpec(memory_space=pltpu.HBM)
    vmem = pl.BlockSpec(memory_space=pltpu.VMEM)
    tiles = (width * rows * chans // LANES, LANES)

    def held(*shape, kind=BF16):
        return pltpu.VMEM(shape, kind)

    sources = (
        packed(fields), packed(cotangent), w_mix, w_up, w_down,
        filters.transpose(0, 2, 1, 3).reshape(3 * KB * rows, TAPS), reach,
    )
    sources = [pltpu.with_memory_space_constraint(source, pltpu.HBM) for source in sources]
    result, grads, back, held_mix, done = pl.pallas_call(
        functools.partial(forward_kernel, width),
        name="halo_forward",
        out_shape=(
            held(*tiles),
            held(rows + 2, RING, chans),
            held(rows, KB * OUTC, 3 * RING),
            held(chans, KB * chans),
            held(2 * OUTC, chans, kind=F32),
        ),
        in_specs=[hbm] * 7,
        out_specs=(vmem,) * 5,
        scratch_shapes=[
            held(*tiles),
            held(*tiles),
            held(*tiles, kind=F32),
            held(3 * KB * rows, TAPS),
            held(3 * KB * rows, TAPS, kind=F32),
            pltpu.SMEM((rows,), jnp.int32),
            held(8, width, chans),
            held(rows, WIDE, chans),
            held(rows, REACH, chans),
            held(rows, REACH, chans),
            held(2, 16, RING),
            held(3, width, chans),
            held(3, width, chans),
            held(16, RING),
            held(16, RING),
            held(rows, WIDE, chans),
            held(rows, WIDE, chans),
            held(rows, REACH, chans),
            held(rows, REACH, chans),
            held(2, WIDE, chans),
            held(2, WIDE, chans),
            held(REACH, chans),
            held(REACH, chans),
            held(2, WIDE, chans),
            held(2, WIDE, chans),
            held(REACH, chans),
            held(REACH, chans),
            held(rows + 4, RING, chans),
            held(rows + 2, CELLS, chans),
            held(rows + 2, 16, RING, kind=F32),
            held(rows + 2, 16, RING, kind=F32),
            held(rows + 2, KB * CELLS, 3 * RING),
            held(2, KB * CELLS, chans, kind=F32),
            held(chans, HID),
            held(HID, chans),
            pltpu.SemaphoreType.DMA((7,)),
            pltpu.SemaphoreType.DMA((16,)),
            pltpu.SemaphoreType.DMA((16,)),
        ],
        compiler_params=pltpu.CompilerParams(
            collective_id=0, has_side_effects=True, vmem_limit_bytes=24 << 20
        ),
    )(*sources)
    result, field_grad = pl.pallas_call(
        functools.partial(backward_kernel, width),
        name="transposed_mix",
        out_shape=(pltpu.HBM(tiles, BF16), pltpu.HBM(tiles, BF16)),
        in_specs=[vmem] * 5,
        out_specs=(hbm, hbm),
        scratch_shapes=[
            held(*tiles, kind=F32),
            held(*tiles),
            pltpu.SemaphoreType.DMA((2,)),
        ],
        compiler_params=pltpu.CompilerParams(vmem_limit_bytes=16 << 20),
    )(result, grads, back, held_mix, done)
    return unpacked(result, rows, width, chans), unpacked(field_grad, rows, width, chans)


def solution(mesh):
    return jax.shard_map(
        on_device,
        mesh=mesh,
        in_specs=(
            P("lat", "lon", None),
            P(),
            P(None, "lat", None, None),
            P("lat"),
            P(),
            P(),
            P("lat", "lon", None),
        ),
        out_specs=(P("lat", "lon", None), P("lat", "lon", None)),
        check_vma=False,
    )
```

```python
import functools

import jax
import jax.numpy as jnp
from jax import lax
from jax.experimental import pallas as pl
from jax.experimental.pallas import tpu as pltpu
from jax.sharding import PartitionSpec as P

KB = 4
REACH = 8
TAPS = 2 * REACH + 1
WIDE = 2 * REACH
CH = 256
HID = 512
ROWS = 4
LANES = 128
RING = 128
CELLS = 112
OUTC = 96
MESH = pl.DeviceIdType.MESH
F32 = jnp.float32
BF16 = jnp.bfloat16


def dot(left, right):
    return jnp.dot(left, right, preferred_element_type=F32)


def dot_last(left, right):
    return lax.dot_general(left, right, (((1,), (1,)), ((), ())), preferred_element_type=F32)


def circulant(taps, count, start):
    spread = jnp.broadcast_to(taps, (count, RING))
    return pltpu.roll(spread, (start - REACH) % RING, 1, stride=1, stride_axis=0)


def packed(grid):
    rows, width, chans = grid.shape
    tiles = grid.transpose(1, 0, 2).reshape(width, rows, chans // LANES, LANES)
    return tiles.transpose(0, 2, 1, 3).reshape(width * rows * chans // LANES, LANES)


def unpacked(tiles, rows, width, chans):
    grid = tiles.reshape(width, chans // LANES, rows, LANES).transpose(0, 2, 1, 3)
    return grid.reshape(width, rows, chans).transpose(1, 0, 2)


def read_row(tiles, row, width):
    return jnp.concatenate(
        [tiles[pl.ds(half * ROWS + row, width, stride=2 * ROWS), :] for half in range(2)], axis=1
    )


def write_row(tiles, row, width, value):
    for half in range(2):
        tiles[pl.ds(half * ROWS + row, width, stride=2 * ROWS), :] = value[
            :, half * LANES : (half + 1) * LANES
        ]


def place():
    lat, lon = lax.axis_index("lat"), lax.axis_index("lon")
    lats, lons = lax.axis_size("lat"), lax.axis_size("lon")
    odd = lax.rem(lat, 2)
    near = jnp.where(odd == 1, lat - 1, lat + 1)
    far = jnp.where(odd == 1, lat + 1, lat - 1)
    has_far = jnp.logical_and(far >= 0, far < lats)
    west = lax.rem(lon + lons - 1, lons)
    east = lax.rem(lon + 1, lons)
    return lat, lon, odd, near, far, has_far, west, east


def owned(odd, row):
    return jnp.where(odd == 1, row, ROWS - 1 - row)


def forward_kernel(
    width,
    fields_hbm, cot_hbm, w_mix_hbm, w_up_hbm, w_down_hbm, filters_hbm, reach_hbm,
    result_ref, grads_ref, back_ref, w_mix, done_ref,
    raw, raw_cot, wide, filters_ref, filters_wide, reach_ref,
    own, edge, cot_w, cot_e, taps_own, near_in, far_in, taps_near, taps_far,
    w_in, e_in, cw_in, ce_in, nw_in, ne_in, ncw_in, nce_in, fw_in, fe_in, fcw_in, fce_in,
    cells, cots, taps, taps_rev, fwd, partial_ref, w_up, w_down,
    load_sem, send_sem, recv_sem, told,
):
    lat, lon, odd, near, far, has_far, west, east = place()

    barrier = pltpu.get_barrier_semaphore()
    lons = lax.axis_size("lon")
    even = odd == 0
    upper = lax.rem(lat, 4) >= 2
    even_lat = lat - odd
    desk = even_lat + 1
    far_even = far - lax.rem(far, 2)
    origin = jnp.logical_and(lat == 0, lon == 0)
    origin_mate = jnp.logical_and(lat == 1, lon == 0)
    beside = jnp.logical_or(lon == 1, lon == lons - 1)
    beside_desk = jnp.logical_and(lat == 1, beside)
    beside_even = jnp.logical_and(lat == 0, beside)
    mate = (near, lon)
    root = (0, 0)

    def both(left, right):
        return jnp.logical_and(left, right)

    def no(flag):
        return jnp.logical_not(flag)

    def greet(target):
        pl.semaphore_signal(barrier, inc=1, device_id=target, device_id_type=MESH)

    def tell(index):
        pl.semaphore_signal(told.at[index], inc=1, device_id=mate, device_id_type=MESH)

    @pl.when(both(no(origin), no(origin_mate)))
    def _():
        greet(mate)

    @pl.when(no(origin))
    def _():
        greet((desk, west))
        greet((desk, east))

    @pl.when(has_far)
    def _():
        for target in ((far_even, lon), (far_even, west), (far_even, east)):
            greet(target)

    fars = jnp.where(even_lat > 0, 1, 0) + jnp.where(desk < lax.axis_size("lat") - 1, 1, 0)
    even_count = 1 + 3 * fars + jnp.where(origin, 2, 0)
    odd_count = 5 - jnp.where(jnp.logical_or(origin_mate, beside_desk), 1, 0)

    loads = [
        (fields_hbm, raw), (cot_hbm, raw_cot), (filters_hbm, filters_ref), (reach_hbm, reach_ref),
        (w_mix_hbm, w_mix), (w_up_hbm, w_up), (w_down_hbm, w_down),
    ]
    loads = [pltpu.make_async_copy(s, d, load_sem.at[i]) for i, (s, d) in enumerate(loads)]
    for load in loads:
        load.start()

    for load, source, slots in ((loads[0], raw, (1, 2, 3, 4)), (loads[1], raw_cot, (0, 6, 7, 5))):
        load.wait()
        wide[...] = source[...].astype(F32)
        for row in range(ROWS):
            own[slots[row]] = read_row(wide, owned(odd, row), width).astype(BF16)

    loads[2].wait()
    loads[3].wait()
    taps[...] = jnp.zeros_like(taps)
    filters_wide[...] = filters_ref[...].astype(F32)
    lane = lax.broadcasted_iota(jnp.int32, (1, TAPS), 1) - REACH
    for row in range(ROWS):
        keep = jnp.abs(lane) <= reach_ref[owned(odd, row)]
        lines = filters_wide[pl.ds(owned(odd, row), 3 * KB, stride=ROWS), :]
        taps[1 + row, 0 : 3 * KB, 0:TAPS] = jnp.where(keep, lines, 0.0)
    taps_own[0] = taps[1].astype(BF16)
    taps_own[1] = taps[ROWS].astype(BF16)

    edge[...] = own[1:5, width - WIDE : width]
    for row, slot in enumerate((0, 6, 7, 5)):
        cot_w[row] = own[slot, 0:REACH]
        cot_e[row] = own[slot, width - REACH : width]

    def remote(index, source, target, device, arrive=None):
        return pltpu.make_async_remote_copy(
            src_ref=source, dst_ref=target, send_sem=send_sem.at[index],
            recv_sem=recv_sem.at[index if arrive is None else arrive], device_id=device, device_id_type=MESH,
        )

    head = pl.ds(0, WIDE)
    far_sends = [
        remote(0, taps_own.at[1], taps_far, (far, lon)),
        remote(1, own.at[pl.ds(3, 2)], far_in.at[pl.ds(0, 2)], (far, lon)),
        remote(2, own.at[pl.ds(3, 2), head], fe_in, (far, west)),
        remote(3, cot_w.at[3], fce_in, (far, west)),
        remote(4, edge.at[pl.ds(2, 2)], fw_in, (far, east)),
        remote(5, cot_e.at[3], fcw_in, (far, east)),
        remote(16, own.at[5], far_in.at[2], (far, lon)),
    ]
    west_sends = [
        remote(6, own.at[pl.ds(1, 4), head], e_in, (lat, west)),
        remote(7, cot_w, ce_in, (lat, west)),
    ]
    east_sends = [
        remote(8, edge, w_in, (lat, east)),
        remote(9, cot_e, cw_in, (lat, east)),
    ]
    mate_sends = [
        remote(10, taps_own.at[0], taps_near, mate),
        remote(11, own.at[pl.ds(0, 3)], near_in, mate),
    ]
    corner_sends = [
        remote(12, e_in.at[pl.ds(0, 2)], ne_in, mate),
        remote(13, ce_in.at[0], nce_in, mate),
        remote(14, w_in.at[pl.ds(0, 2)], nw_in, mate),
        remote(15, cw_in.at[0], ncw_in, mate),
    ]
    corner_west_sends = [
        remote(17, own.at[pl.ds(1, 2), head], ne_in, (near, west), 12),
        remote(18, cot_w.at[0], nce_in, (near, west), 13),
    ]
    corner_east_sends = [
        remote(19, edge.at[pl.ds(0, 2)], nw_in, (near, east), 14),
        remote(20, cot_e.at[0], ncw_in, (near, east), 15),
    ]
    corner_west = both(beside_even, lon == 1)
    corner_east = both(beside_even, lon == lons - 1)
    groups = (west_sends, east_sends, mate_sends)
    lon_sends = west_sends + east_sends
    near_sends = mate_sends + corner_sends

    def start(copies):
        for copy in copies:
            copy.start()

    def start_sides():
        west_last, east_last = lon == 1, lon == lons - 1
        pl.when(no(both(beside_even, west_last)))(functools.partial(start, west_sends))
        pl.when(no(both(beside_even, east_last)))(functools.partial(start, east_sends))
        pl.when(corner_west)(functools.partial(start, corner_west_sends))
        pl.when(corner_east)(functools.partial(start, corner_east_sends))

    @pl.when(origin)
    def _():
        pl.semaphore_wait(barrier, even_count)
        for target in ((1, 0), (1, 1), (1, lons - 1)):
            greet(target)

    @pl.when(jnp.logical_and(upper, even))
    def _():
        pl.semaphore_wait(barrier, even_count)
        tell(0)

    @pl.when(jnp.logical_and(no(upper), no(even)))
    def _():
        pl.semaphore_wait(barrier, odd_count)
        pl.when(jnp.logical_or(origin_mate, beside_desk))(functools.partial(greet, root))
        pl.when(no(origin_mate))(functools.partial(tell, 0))

    @pl.when(upper == (odd == 1))
    def _():
        pl.semaphore_wait(told.at[0], 1)

    pl.when(both(upper, has_far))(functools.partial(start, far_sends[2:6] + far_sends[:1]))
    pl.when(no(upper))(start_sides)
    pl.when(no(origin_mate))(functools.partial(start, mate_sends))

    @pl.when(origin_mate)
    def _():
        pl.semaphore_wait(barrier, 1)
        tell(0)
        start(mate_sends)

    @pl.when(jnp.logical_not(has_far))
    def _():
        for ref in (far_in, taps_far, fe_in, fce_in, fw_in, fcw_in):
            ref[...] = jnp.zeros_like(ref)

    first = lax.broadcasted_iota(jnp.int32, (RING, RING), 0)
    second = lax.broadcasted_iota(jnp.int32, (RING, RING), 1)
    flip = (first + second == 2 * REACH).astype(BF16)

    def tap_line(tap, basis):
        return basis * 3 + jnp.where(odd == 1, tap, 2 - tap)

    def reverse(row):
        taps_rev[row + 1] = dot(taps[row + 1].astype(BF16), flip)

    def forward_matrix(row):
        for tap in range(3):
            for basis in range(KB):
                line = taps[row + 1, pl.ds(tap_line(tap, basis), 1), :]
                block = jnp.concatenate(
                    [circulant(line, 104, 0), circulant(line, REACH, RING - REACH)], axis=0
                )
                fwd[row + 1, basis * CELLS : (basis + 1) * CELLS, tap * RING : (tap + 1) * RING] = (
                    block.astype(BF16)
                )

    def backward_blocks(source):
        for out in range(max(0, source - 1), min(ROWS, source + 2)):
            tap, slot = out - source + 1, source - out + 1
            for basis in range(KB):
                line = taps_rev[source + 1, pl.ds(tap_line(tap, basis), 1), :]
                back_ref[out, basis * OUTC : (basis + 1) * OUTC, slot * RING : (slot + 1) * RING] = (
                    circulant(line, OUTC, 0).astype(BF16)
                )

    for row in range(ROWS):
        reverse(row)
        forward_matrix(row)
        backward_blocks(row)

    @pl.when(both(no(upper), even))
    def _():
        pl.when(no(origin))(lambda: pl.semaphore_wait(barrier, even_count))
        tell(1)

    @pl.when(both(upper, no(even)))
    def _():
        pl.semaphore_wait(barrier, odd_count)
        tell(1)

    @pl.when(upper == even)
    def _():
        pl.semaphore_wait(told.at[1], 1)

    pl.when(both(no(upper), has_far))(
        functools.partial(start, far_sends[2:6] + far_sends[:2] + far_sends[6:])
    )

    pl.when(upper)(start_sides)
    pl.when(both(upper, has_far))(functools.partial(start, far_sends[1:2] + far_sends[6:]))

    @pl.when(beside_desk)
    def _():
        pl.semaphore_wait(barrier, 1)
        tell(2)

    @pl.when(beside_even)
    def _():
        pl.semaphore_wait(told.at[2], 1)
        pl.when(lon == 1)(functools.partial(start, west_sends))
        pl.when(lon == lons - 1)(functools.partial(start, east_sends))

    for load in loads[4:]:
        load.wait()

    def fill_cells(row, middle, west_part, east_part):
        cells[row + 2, 0:width] = middle
        cells[row + 2, width : width + WIDE] = east_part
        cells[row + 2, width + WIDE : RING - WIDE] = jnp.zeros(
            (RING - 2 * WIDE - width, CH), BF16
        )
        cells[row + 2, RING - WIDE : RING] = west_part

    def fill_cots(row, middle, west_part, east_part):
        cots[row + 1, 0:width] = middle
        cots[row + 1, width : width + REACH] = east_part
        cots[row + 1, width + REACH : 104] = jnp.zeros((104 - REACH - width, CH), BF16)
        cots[row + 1, 104:CELLS] = west_part

    def conv_part(row, begin, end):
        source = cells[row + 1 + begin : row + 1 + end].reshape((end - begin) * RING, CH)
        return dot(fwd[row + 1, :, begin * RING : end * RING], source)

    def advance(rows, ready=None):
        count = len(rows)
        convs = []
        for n, row in enumerate(rows):
            if ready is None:
                conv = conv_part(row, 0, 3)
            else:
                conv = partial_ref[n] + conv_part(row, ready[n], 3)
            convs.append(conv.astype(BF16))
        spatial = jnp.zeros((count * CELLS, CH), F32)
        for basis in range(KB):
            part = jnp.concatenate(
                [c[basis * CELLS : (basis + 1) * CELLS] for c in convs], axis=0
            )
            spatial = spatial + dot(part, w_mix[:, basis * CH : (basis + 1) * CH])
        centre = jnp.concatenate(
            [p for row in rows for p in (cells[row + 2, 0:104].astype(F32), cells[row + 2, 120:128].astype(F32))],
            axis=0,
        )
        hidden = (centre + spatial).astype(BF16)
        pre = dot(hidden, w_up[...])
        half = 0.5 * (1.0 + lax.erf(pre * 0.7071067811865476))
        slope = half + pre * jnp.exp(-0.5 * pre * pre) * 0.3989422804014327
        upstream = jnp.concatenate([cots[row + 1] for row in rows], axis=0)
        grad_active = (dot_last(upstream, w_down[...]) * slope).astype(BF16)
        grad = (upstream.astype(F32) + dot_last(grad_active, w_up[...])).astype(BF16)
        active = (half * pre).astype(BF16)
        for n, row in enumerate(rows):
            base = n * CELLS
            grads_ref[row + 1, 0:104] = grad[base : base + 104]
            grads_ref[row + 1, 104:120] = jnp.zeros((WIDE, CH), BF16)
            grads_ref[row + 1, 120:128] = grad[base + 104 : base + CELLS]
            if 0 <= row < ROWS:
                result = hidden[base : base + OUTC].astype(F32) + dot(
                    active[base : base + OUTC], w_down[...]
                )
                write_row(wide, owned(odd, row), width, result[:width])

    def finish(rows):
        return retreat(rows, grads_ref, back_ref, w_mix)

    for copy in lon_sends:
        copy.wait_recv()
    pl.when(no(origin))(functools.partial(start, corner_sends))
    for row in range(ROWS):
        fill_cells(row, own[1 + row], w_in[row], e_in[row])
        fill_cots(row, own[(0, 6, 7, 5)[row]], cw_in[row], ce_in[row])
    advance((1, 2))

    mate_sends[0].wait_recv()
    taps[0] = taps_near[...].astype(F32)
    reverse(-1)
    forward_matrix(-1)
    backward_blocks(-1)
    for copy in near_sends[1:]:
        copy.wait_recv()
    fill_cells(-1, near_in[1], nw_in[0], ne_in[0])
    fill_cells(-2, near_in[2], nw_in[1], ne_in[1])
    fill_cots(-1, near_in[0], ncw_in[...], nce_in[...])
    advance((0, -1))
    done_ref[...] = finish((0, 1))

    pl.when(has_far)(far_sends[0].wait_recv)
    taps[ROWS + 1] = taps_far[...].astype(F32)
    reverse(ROWS)
    forward_matrix(ROWS)
    backward_blocks(ROWS)
    partial_ref[0] = conv_part(ROWS - 1, 0, 2)
    partial_ref[1] = conv_part(ROWS, 0, 1)

    @pl.when(has_far)
    def _():
        for copy in far_sends[1:]:
            copy.wait_recv()

    fill_cells(ROWS, far_in[1], fw_in[1], fe_in[1])
    fill_cells(ROWS + 1, far_in[0], fw_in[0], fe_in[0])
    fill_cots(ROWS, far_in[2], fcw_in[...], fce_in[...])
    advance((ROWS - 1, ROWS), ready=(2, 1))
    result_ref[...] = wide[...].astype(BF16)

    def drain(copies):
        for copy in copies:
            copy.wait_send()

    for copies in groups:
        drain(copies)
    pl.when(no(origin))(functools.partial(drain, corner_sends))
    pl.when(corner_west)(functools.partial(drain, corner_west_sends))
    pl.when(corner_east)(functools.partial(drain, corner_east_sends))

    @pl.when(has_far)
    def _():
        for copy in far_sends:
            copy.wait_send()


def retreat(rows, grads_ref, back_ref, w_mix):
    convs = []
    for row in rows:
        source = grads_ref[row : row + 3].reshape(3 * RING, CH)
        convs.append(dot(back_ref[row], source).astype(BF16))
    total = jnp.concatenate([grads_ref[row + 1, 0:OUTC].astype(F32) for row in rows], axis=0)
    for basis in range(KB):
        part = jnp.concatenate([c[basis * OUTC : (basis + 1) * OUTC] for c in convs], axis=0)
        total = total + dot_last(part, w_mix[:, basis * CH : (basis + 1) * CH])
    return total


def backward_kernel(
    width, packed_result, grads_ref, back_ref, w_mix, done_ref, result_hbm, grad_hbm, wide, out, sems
):
    odd = lax.rem(lax.axis_index("lat"), 2)
    store_result = pltpu.make_async_copy(packed_result, result_hbm, sems.at[0])
    store_result.start()
    total = retreat((2, 3), grads_ref, back_ref, w_mix)
    for row in (0, 1):
        write_row(wide, owned(odd, row), width, done_ref[row * OUTC : row * OUTC + width])
        write_row(wide, owned(odd, 2 + row), width, total[row * OUTC : row * OUTC + width])
    out[...] = wide[...].astype(BF16)
    store_grad = pltpu.make_async_copy(out, grad_hbm, sems.at[1])
    store_grad.start()
    store_result.wait()
    store_grad.wait()


def on_device(fields, w_mix, filters, reach, w_up, w_down, cotangent):
    rows, width, chans = fields.shape
    hbm = pl.BlockSpec(memory_space=pltpu.HBM)
    vmem = pl.BlockSpec(memory_space=pltpu.VMEM)
    tiles = (width * rows * chans // LANES, LANES)

    def held(*shape, kind=BF16):
        return pltpu.VMEM(shape, kind)

    sources = (
        packed(fields), packed(cotangent), w_mix, w_up, w_down,
        filters.transpose(0, 2, 1, 3).reshape(3 * KB * rows, TAPS), reach,
    )
    sources = [pltpu.with_memory_space_constraint(source, pltpu.HBM) for source in sources]
    result, grads, back, held_mix, done = pl.pallas_call(
        functools.partial(forward_kernel, width),
        name="halo_forward",
        out_shape=(
            held(*tiles),
            held(rows + 2, RING, chans),
            held(rows, KB * OUTC, 3 * RING),
            held(chans, KB * chans),
            held(2 * OUTC, chans, kind=F32),
        ),
        in_specs=[hbm] * 7,
        out_specs=(vmem,) * 5,
        scratch_shapes=[
            held(*tiles),
            held(*tiles),
            held(*tiles, kind=F32),
            held(3 * KB * rows, TAPS),
            held(3 * KB * rows, TAPS, kind=F32),
            pltpu.SMEM((rows,), jnp.int32),
            held(8, width, chans),
            held(rows, WIDE, chans),
            held(rows, REACH, chans),
            held(rows, REACH, chans),
            held(2, 16, RING),
            held(3, width, chans),
            held(3, width, chans),
            held(16, RING),
            held(16, RING),
            held(rows, WIDE, chans),
            held(rows, WIDE, chans),
            held(rows, REACH, chans),
            held(rows, REACH, chans),
            held(2, WIDE, chans),
            held(2, WIDE, chans),
            held(REACH, chans),
            held(REACH, chans),
            held(2, WIDE, chans),
            held(2, WIDE, chans),
            held(REACH, chans),
            held(REACH, chans),
            held(rows + 4, RING, chans),
            held(rows + 2, CELLS, chans),
            held(rows + 2, 16, RING, kind=F32),
            held(rows + 2, 16, RING, kind=F32),
            held(rows + 2, KB * CELLS, 3 * RING),
            held(2, KB * CELLS, chans, kind=F32),
            held(chans, HID),
            held(HID, chans),
            pltpu.SemaphoreType.DMA((7,)),
            pltpu.SemaphoreType.DMA((21,)),
            pltpu.SemaphoreType.DMA((17,)),
            pltpu.SemaphoreType.REGULAR((3,)),
        ],
        compiler_params=pltpu.CompilerParams(
            collective_id=0, has_side_effects=True, vmem_limit_bytes=24 << 20
        ),
    )(*sources)
    result, field_grad = pl.pallas_call(
        functools.partial(backward_kernel, width),
        name="transposed_mix",
        out_shape=(pltpu.HBM(tiles, BF16), pltpu.HBM(tiles, BF16)),
        in_specs=[vmem] * 5,
        out_specs=(hbm, hbm),
        scratch_shapes=[
            held(*tiles, kind=F32),
            held(*tiles),
            pltpu.SemaphoreType.DMA((2,)),
        ],
        compiler_params=pltpu.CompilerParams(vmem_limit_bytes=16 << 20),
    )(result, grads, back, held_mix, done)
    return unpacked(result, rows, width, chans), unpacked(field_grad, rows, width, chans)


def solution(mesh):
    return jax.shard_map(
        on_device,
        mesh=mesh,
        in_specs=(
            P("lat", "lon", None),
            P(),
            P(None, "lat", None, None),
            P("lat"),
            P(),
            P(),
            P("lat", "lon", None),
        ),
        out_specs=(P("lat", "lon", None), P("lat", "lon", None)),
        check_vma=False,
    )
```

```python
import functools

import jax
import jax.numpy as jnp
from jax import lax
from jax.experimental import pallas as pl
from jax.experimental.pallas import tpu as pltpu
from jax.sharding import PartitionSpec as P

KB = 4
REACH = 8
TAPS = 2 * REACH + 1
WIDE = 2 * REACH
CH = 256
HID = 512
ROWS = 4
LANES = 128
RING = 128
CELLS = 112
OUTC = 96
MESH = pl.DeviceIdType.MESH
F32 = jnp.float32
BF16 = jnp.bfloat16


def dot(left, right):
    return jnp.dot(left, right, preferred_element_type=F32)


def dot_last(left, right):
    return lax.dot_general(left, right, (((1,), (1,)), ((), ())), preferred_element_type=F32)


def circulant(taps, count, start):
    spread = jnp.broadcast_to(taps, (count, RING))
    return pltpu.roll(spread, (start - REACH) % RING, 1, stride=1, stride_axis=0)


def packed(grid):
    rows, width, chans = grid.shape
    tiles = grid.transpose(1, 0, 2).reshape(width, rows, chans // LANES, LANES)
    return tiles.transpose(0, 2, 1, 3).reshape(width * rows * chans // LANES, LANES)


def unpacked(tiles, rows, width, chans):
    grid = tiles.reshape(width, chans // LANES, rows, LANES).transpose(0, 2, 1, 3)
    return grid.reshape(width, rows, chans).transpose(1, 0, 2)


def read_row(tiles, row, width):
    return jnp.concatenate(
        [tiles[pl.ds(half * ROWS + row, width, stride=2 * ROWS), :] for half in range(2)], axis=1
    )


def write_row(tiles, row, width, value):
    for half in range(2):
        tiles[pl.ds(half * ROWS + row, width, stride=2 * ROWS), :] = value[
            :, half * LANES : (half + 1) * LANES
        ]


def place():
    lat, lon = lax.axis_index("lat"), lax.axis_index("lon")
    lats, lons = lax.axis_size("lat"), lax.axis_size("lon")
    odd = lax.rem(lat, 2)
    near = jnp.where(odd == 1, lat - 1, lat + 1)
    far = jnp.where(odd == 1, lat + 1, lat - 1)
    has_far = jnp.logical_and(far >= 0, far < lats)
    west = lax.rem(lon + lons - 1, lons)
    east = lax.rem(lon + 1, lons)
    return lat, lon, odd, near, far, has_far, west, east


def owned(odd, row):
    return jnp.where(odd == 1, row, ROWS - 1 - row)


def forward_kernel(
    width,
    fields_hbm, cot_hbm, w_mix_hbm, w_up_hbm, w_down_hbm, filters_hbm, reach_hbm,
    result_ref, grads_ref, back_ref, w_mix, done_ref,
    raw, raw_cot, wide, filters_ref, filters_wide, reach_ref,
    own, edge, cot_w, cot_e, taps_own, near_in, far_in, taps_near, taps_far,
    w_in, e_in, cw_in, ce_in, nw_in, ne_in, ncw_in, nce_in, fw_in, fe_in, fcw_in, fce_in,
    cells, cots, taps, taps_rev, fwd, partial_ref, w_up, w_down,
    load_sem, send_sem, recv_sem, told,
):
    lat, lon, odd, near, far, has_far, west, east = place()

    barrier = pltpu.get_barrier_semaphore()
    lons = lax.axis_size("lon")
    even = odd == 0
    upper = lax.rem(lat, 4) >= 2
    even_lat = lat - odd
    desk = even_lat + 1
    far_even = far - lax.rem(far, 2)
    origin = jnp.logical_and(lat == 0, lon == 0)
    origin_mate = jnp.logical_and(lat == 1, lon == 0)
    beside = jnp.logical_or(lon == 1, lon == lons - 1)
    beside_desk = jnp.logical_and(lat == 1, beside)
    beside_even = jnp.logical_and(lat == 0, beside)
    mate = (near, lon)
    root = (0, 0)

    def both(left, right):
        return jnp.logical_and(left, right)

    def no(flag):
        return jnp.logical_not(flag)

    def greet(target):
        pl.semaphore_signal(barrier, inc=1, device_id=target, device_id_type=MESH)

    def tell(index):
        pl.semaphore_signal(told.at[index], inc=1, device_id=mate, device_id_type=MESH)

    @pl.when(both(no(origin), no(origin_mate)))
    def _():
        greet(mate)

    @pl.when(no(origin))
    def _():
        greet((desk, west))
        greet((desk, east))

    @pl.when(has_far)
    def _():
        for target in ((far_even, lon), (far_even, west), (far_even, east)):
            greet(target)

    fars = jnp.where(even_lat > 0, 1, 0) + jnp.where(desk < lax.axis_size("lat") - 1, 1, 0)
    even_count = 1 + 3 * fars + jnp.where(origin, 2, 0)
    odd_count = 5 - jnp.where(jnp.logical_or(origin_mate, beside_desk), 1, 0)

    loads = [
        (fields_hbm, raw), (cot_hbm, raw_cot), (filters_hbm, filters_ref), (reach_hbm, reach_ref),
        (w_mix_hbm, w_mix), (w_up_hbm, w_up), (w_down_hbm, w_down),
    ]
    loads = [pltpu.make_async_copy(s, d, load_sem.at[i]) for i, (s, d) in enumerate(loads)]
    for load in loads:
        load.start()

    for load, source, slots in ((loads[0], raw, (1, 2, 3, 4)), (loads[1], raw_cot, (0, 6, 7, 5))):
        load.wait()
        wide[...] = source[...].astype(F32)
        for row in range(ROWS):
            own[slots[row]] = read_row(wide, owned(odd, row), width).astype(BF16)

    loads[2].wait()
    loads[3].wait()
    taps[...] = jnp.zeros_like(taps)
    filters_wide[...] = filters_ref[...].astype(F32)
    lane = lax.broadcasted_iota(jnp.int32, (1, TAPS), 1) - REACH
    for row in range(ROWS):
        keep = jnp.abs(lane) <= reach_ref[owned(odd, row)]
        lines = filters_wide[pl.ds(owned(odd, row), 3 * KB, stride=ROWS), :]
        taps[1 + row, 0 : 3 * KB, 0:TAPS] = jnp.where(keep, lines, 0.0)
    taps_own[0] = taps[1].astype(BF16)
    taps_own[1] = taps[ROWS].astype(BF16)

    edge[...] = own[1:5, width - WIDE : width]
    for row, slot in enumerate((0, 6, 7, 5)):
        cot_w[row] = own[slot, 0:REACH]
        cot_e[row] = own[slot, width - REACH : width]

    def remote(index, source, target, device, arrive=None):
        return pltpu.make_async_remote_copy(
            src_ref=source, dst_ref=target, send_sem=send_sem.at[index],
            recv_sem=recv_sem.at[index if arrive is None else arrive], device_id=device, device_id_type=MESH,
        )

    head = pl.ds(0, WIDE)
    far_sends = [
        remote(0, taps_own.at[1], taps_far, (far, lon)),
        remote(1, own.at[pl.ds(3, 2)], far_in.at[pl.ds(0, 2)], (far, lon)),
        remote(2, own.at[pl.ds(3, 2), head], fe_in, (far, west)),
        remote(3, cot_w.at[3], fce_in, (far, west)),
        remote(4, edge.at[pl.ds(2, 2)], fw_in, (far, east)),
        remote(5, cot_e.at[3], fcw_in, (far, east)),
        remote(16, own.at[5], far_in.at[2], (far, lon)),
    ]
    west_sends = [
        remote(6, own.at[pl.ds(1, 4), head], e_in, (lat, west)),
        remote(7, cot_w, ce_in, (lat, west)),
    ]
    east_sends = [
        remote(8, edge, w_in, (lat, east)),
        remote(9, cot_e, cw_in, (lat, east)),
    ]
    mate_sends = [
        remote(10, taps_own.at[0], taps_near, mate),
        remote(11, own.at[pl.ds(0, 3)], near_in, mate),
    ]
    corner_sends = [
        remote(12, e_in.at[pl.ds(0, 2)], ne_in, mate),
        remote(13, ce_in.at[0], nce_in, mate),
        remote(14, w_in.at[pl.ds(0, 2)], nw_in, mate),
        remote(15, cw_in.at[0], ncw_in, mate),
    ]
    corner_west_sends = [
        remote(17, own.at[pl.ds(1, 2), head], ne_in, (near, west), 12),
        remote(18, cot_w.at[0], nce_in, (near, west), 13),
    ]
    corner_east_sends = [
        remote(19, edge.at[pl.ds(0, 2)], nw_in, (near, east), 14),
        remote(20, cot_e.at[0], ncw_in, (near, east), 15),
    ]
    corner_west = both(beside_even, lon == 1)
    corner_east = both(beside_even, lon == lons - 1)
    groups = (west_sends, east_sends, mate_sends)
    lon_sends = west_sends + east_sends
    near_sends = mate_sends + corner_sends

    def start(copies):
        for copy in copies:
            copy.start()

    def start_sides():
        west_last, east_last = lon == 1, lon == lons - 1
        pl.when(no(both(beside_even, west_last)))(functools.partial(start, west_sends))
        pl.when(no(both(beside_even, east_last)))(functools.partial(start, east_sends))
        pl.when(corner_west)(functools.partial(start, corner_west_sends))
        pl.when(corner_east)(functools.partial(start, corner_east_sends))

    @pl.when(origin)
    def _():
        pl.semaphore_wait(barrier, even_count)
        for target in ((1, 0), (1, 1), (1, lons - 1)):
            greet(target)

    @pl.when(jnp.logical_and(upper, even))
    def _():
        pl.semaphore_wait(barrier, even_count)
        tell(0)

    @pl.when(jnp.logical_and(no(upper), no(even)))
    def _():
        pl.semaphore_wait(barrier, odd_count)
        pl.when(jnp.logical_or(origin_mate, beside_desk))(functools.partial(greet, root))
        pl.when(no(origin_mate))(functools.partial(tell, 0))

    @pl.when(upper == (odd == 1))
    def _():
        pl.semaphore_wait(told.at[0], 1)

    pl.when(both(upper, has_far))(functools.partial(start, far_sends[2:6] + far_sends[:1]))
    pl.when(no(upper))(start_sides)
    pl.when(no(origin_mate))(functools.partial(start, mate_sends))

    @pl.when(origin_mate)
    def _():
        pl.semaphore_wait(barrier, 1)
        tell(0)
        start(mate_sends)

    @pl.when(jnp.logical_not(has_far))
    def _():
        for ref in (far_in, taps_far, fe_in, fce_in, fw_in, fcw_in):
            ref[...] = jnp.zeros_like(ref)

    first = lax.broadcasted_iota(jnp.int32, (RING, RING), 0)
    second = lax.broadcasted_iota(jnp.int32, (RING, RING), 1)
    flip = (first + second == 2 * REACH).astype(BF16)

    def tap_line(tap, basis):
        return basis * 3 + jnp.where(odd == 1, tap, 2 - tap)

    def reverse(row):
        taps_rev[row + 1] = dot(taps[row + 1].astype(BF16), flip)

    def forward_matrix(row):
        for tap in range(3):
            for basis in range(KB):
                line = taps[row + 1, pl.ds(tap_line(tap, basis), 1), :]
                block = jnp.concatenate(
                    [circulant(line, 104, 0), circulant(line, REACH, RING - REACH)], axis=0
                )
                fwd[row + 1, basis * CELLS : (basis + 1) * CELLS, tap * RING : (tap + 1) * RING] = (
                    block.astype(BF16)
                )

    def backward_blocks(source):
        for out in range(max(0, source - 1), min(ROWS, source + 2)):
            tap, slot = out - source + 1, source - out + 1
            for basis in range(KB):
                line = taps_rev[source + 1, pl.ds(tap_line(tap, basis), 1), :]
                back_ref[out, basis * OUTC : (basis + 1) * OUTC, slot * RING : (slot + 1) * RING] = (
                    circulant(line, OUTC, 0).astype(BF16)
                )

    @pl.when(both(no(upper), even))
    def _():
        pl.when(no(origin))(lambda: pl.semaphore_wait(barrier, even_count))
        tell(1)

    @pl.when(both(upper, no(even)))
    def _():
        pl.semaphore_wait(barrier, odd_count)
        tell(1)

    @pl.when(upper == even)
    def _():
        pl.semaphore_wait(told.at[1], 1)

    pl.when(both(no(upper), has_far))(
        functools.partial(start, far_sends[2:6] + far_sends[:2] + far_sends[6:])
    )

    pl.when(upper)(start_sides)
    pl.when(both(upper, has_far))(functools.partial(start, far_sends[1:2] + far_sends[6:]))

    @pl.when(beside_desk)
    def _():
        pl.semaphore_wait(barrier, 1)
        tell(2)

    @pl.when(beside_even)
    def _():
        pl.semaphore_wait(told.at[2], 1)
        pl.when(lon == 1)(functools.partial(start, west_sends))
        pl.when(lon == lons - 1)(functools.partial(start, east_sends))

    for row in range(ROWS):
        reverse(row)
        forward_matrix(row)
        backward_blocks(row)

    for load in loads[4:]:
        load.wait()

    def fill_cells(row, middle, west_part, east_part):
        cells[row + 2, 0:width] = middle
        cells[row + 2, width : width + WIDE] = east_part
        cells[row + 2, width + WIDE : RING - WIDE] = jnp.zeros(
            (RING - 2 * WIDE - width, CH), BF16
        )
        cells[row + 2, RING - WIDE : RING] = west_part

    def fill_cots(row, middle, west_part, east_part):
        cots[row + 1, 0:width] = middle
        cots[row + 1, width : width + REACH] = east_part
        cots[row + 1, width + REACH : 104] = jnp.zeros((104 - REACH - width, CH), BF16)
        cots[row + 1, 104:CELLS] = west_part

    def conv_part(row, begin, end):
        source = cells[row + 1 + begin : row + 1 + end].reshape((end - begin) * RING, CH)
        return dot(fwd[row + 1, :, begin * RING : end * RING], source)

    def advance(rows, ready=None, between=None):
        count = len(rows)
        convs = []
        for n, row in enumerate(rows):
            if ready is None:
                conv = conv_part(row, 0, 3)
            else:
                conv = partial_ref[n] + conv_part(row, ready[n], 3)
            convs.append(conv.astype(BF16))
        spatial = jnp.zeros((count * CELLS, CH), F32)
        for basis in range(KB):
            part = jnp.concatenate(
                [c[basis * CELLS : (basis + 1) * CELLS] for c in convs], axis=0
            )
            spatial = spatial + dot(part, w_mix[:, basis * CH : (basis + 1) * CH])
        centre = jnp.concatenate(
            [p for row in rows for p in (cells[row + 2, 0:104].astype(F32), cells[row + 2, 120:128].astype(F32))],
            axis=0,
        )
        hidden = (centre + spatial).astype(BF16)
        pre = dot(hidden, w_up[...])
        half = 0.5 * (1.0 + lax.erf(pre * 0.7071067811865476))
        slope = half + pre * jnp.exp(-0.5 * pre * pre) * 0.3989422804014327
        active = (half * pre).astype(BF16)
        for n, row in enumerate(rows):
            base = n * CELLS
            if 0 <= row < ROWS:
                result = hidden[base : base + OUTC].astype(F32) + dot(
                    active[base : base + OUTC], w_down[...]
                )
                write_row(wide, owned(odd, row), width, result[:width])
        if between is not None:
            between()
        upstream = jnp.concatenate([cots[row + 1] for row in rows], axis=0)
        grad_active = (dot_last(upstream, w_down[...]) * slope).astype(BF16)
        grad = (upstream.astype(F32) + dot_last(grad_active, w_up[...])).astype(BF16)
        for n, row in enumerate(rows):
            base = n * CELLS
            grads_ref[row + 1, 0:104] = grad[base : base + 104]
            grads_ref[row + 1, 104:120] = jnp.zeros((WIDE, CH), BF16)
            grads_ref[row + 1, 120:128] = grad[base + 104 : base + CELLS]

    def finish(rows):
        return retreat(rows, grads_ref, back_ref, w_mix)

    for copy in lon_sends:
        copy.wait_recv()
    pl.when(no(origin))(functools.partial(start, corner_sends))
    for row in range(ROWS):
        fill_cells(row, own[1 + row], w_in[row], e_in[row])
        fill_cots(row, own[(0, 6, 7, 5)[row]], cw_in[row], ce_in[row])
    advance((1, 2))

    mate_sends[0].wait_recv()
    taps[0] = taps_near[...].astype(F32)
    reverse(-1)
    forward_matrix(-1)
    backward_blocks(-1)
    for copy in near_sends[1:]:
        copy.wait_recv()
    fill_cells(-1, near_in[1], nw_in[0], ne_in[0])
    fill_cells(-2, near_in[2], nw_in[1], ne_in[1])
    fill_cots(-1, near_in[0], ncw_in[...], nce_in[...])
    advance((0, -1))
    done_ref[...] = finish((0, 1))

    pl.when(has_far)(far_sends[0].wait_recv)
    taps[ROWS + 1] = taps_far[...].astype(F32)
    reverse(ROWS)
    forward_matrix(ROWS)
    backward_blocks(ROWS)
    partial_ref[0] = conv_part(ROWS - 1, 0, 2)
    partial_ref[1] = conv_part(ROWS, 0, 1)

    @pl.when(has_far)
    def _():
        for copy in far_sends[1:6]:
            copy.wait_recv()

    fill_cells(ROWS, far_in[1], fw_in[1], fe_in[1])
    fill_cells(ROWS + 1, far_in[0], fw_in[0], fe_in[0])

    def last_cots():
        result_ref[...] = wide[...].astype(BF16)
        pl.when(has_far)(far_sends[6].wait_recv)
        fill_cots(ROWS, far_in[2], fcw_in[...], fce_in[...])

    advance((ROWS - 1, ROWS), ready=(2, 1), between=last_cots)

    def drain(copies):
        for copy in copies:
            copy.wait_send()

    for copies in groups:
        drain(copies)
    pl.when(no(origin))(functools.partial(drain, corner_sends))
    pl.when(corner_west)(functools.partial(drain, corner_west_sends))
    pl.when(corner_east)(functools.partial(drain, corner_east_sends))

    @pl.when(has_far)
    def _():
        for copy in far_sends:
            copy.wait_send()


def retreat(rows, grads_ref, back_ref, w_mix):
    convs = []
    for row in rows:
        source = grads_ref[row : row + 3].reshape(3 * RING, CH)
        convs.append(dot(back_ref[row], source).astype(BF16))
    total = jnp.concatenate([grads_ref[row + 1, 0:OUTC].astype(F32) for row in rows], axis=0)
    for basis in range(KB):
        part = jnp.concatenate([c[basis * OUTC : (basis + 1) * OUTC] for c in convs], axis=0)
        total = total + dot_last(part, w_mix[:, basis * CH : (basis + 1) * CH])
    return total


def backward_kernel(
    width, packed_result, grads_ref, back_ref, w_mix, done_ref, result_hbm, grad_hbm, wide, out, sems
):
    odd = lax.rem(lax.axis_index("lat"), 2)
    store_result = pltpu.make_async_copy(packed_result, result_hbm, sems.at[0])
    store_result.start()
    total = retreat((2, 3), grads_ref, back_ref, w_mix)
    for row in (0, 1):
        write_row(wide, owned(odd, row), width, done_ref[row * OUTC : row * OUTC + width])
        write_row(wide, owned(odd, 2 + row), width, total[row * OUTC : row * OUTC + width])
    out[...] = wide[...].astype(BF16)
    store_grad = pltpu.make_async_copy(out, grad_hbm, sems.at[1])
    store_grad.start()
    store_result.wait()
    store_grad.wait()


def on_device(fields, w_mix, filters, reach, w_up, w_down, cotangent):
    rows, width, chans = fields.shape
    hbm = pl.BlockSpec(memory_space=pltpu.HBM)
    vmem = pl.BlockSpec(memory_space=pltpu.VMEM)
    tiles = (width * rows * chans // LANES, LANES)

    def held(*shape, kind=BF16):
        return pltpu.VMEM(shape, kind)

    sources = (
        packed(fields), packed(cotangent), w_mix, w_up, w_down,
        filters.transpose(0, 2, 1, 3).reshape(3 * KB * rows, TAPS), reach,
    )
    sources = [pltpu.with_memory_space_constraint(source, pltpu.HBM) for source in sources]
    result, grads, back, held_mix, done = pl.pallas_call(
        functools.partial(forward_kernel, width),
        name="halo_forward",
        out_shape=(
            held(*tiles),
            held(rows + 2, RING, chans),
            held(rows, KB * OUTC, 3 * RING),
            held(chans, KB * chans),
            held(2 * OUTC, chans, kind=F32),
        ),
        in_specs=[hbm] * 7,
        out_specs=(vmem,) * 5,
        scratch_shapes=[
            held(*tiles),
            held(*tiles),
            held(*tiles, kind=F32),
            held(3 * KB * rows, TAPS),
            held(3 * KB * rows, TAPS, kind=F32),
            pltpu.SMEM((rows,), jnp.int32),
            held(8, width, chans),
            held(rows, WIDE, chans),
            held(rows, REACH, chans),
            held(rows, REACH, chans),
            held(2, 16, RING),
            held(3, width, chans),
            held(3, width, chans),
            held(16, RING),
            held(16, RING),
            held(rows, WIDE, chans),
            held(rows, WIDE, chans),
            held(rows, REACH, chans),
            held(rows, REACH, chans),
            held(2, WIDE, chans),
            held(2, WIDE, chans),
            held(REACH, chans),
            held(REACH, chans),
            held(2, WIDE, chans),
            held(2, WIDE, chans),
            held(REACH, chans),
            held(REACH, chans),
            held(rows + 4, RING, chans),
            held(rows + 2, CELLS, chans),
            held(rows + 2, 16, RING, kind=F32),
            held(rows + 2, 16, RING, kind=F32),
            held(rows + 2, KB * CELLS, 3 * RING),
            held(2, KB * CELLS, chans, kind=F32),
            held(chans, HID),
            held(HID, chans),
            pltpu.SemaphoreType.DMA((7,)),
            pltpu.SemaphoreType.DMA((21,)),
            pltpu.SemaphoreType.DMA((17,)),
            pltpu.SemaphoreType.REGULAR((3,)),
        ],
        compiler_params=pltpu.CompilerParams(
            collective_id=0, has_side_effects=True, vmem_limit_bytes=24 << 20
        ),
    )(*sources)
    result, field_grad = pl.pallas_call(
        functools.partial(backward_kernel, width),
        name="transposed_mix",
        out_shape=(pltpu.HBM(tiles, BF16), pltpu.HBM(tiles, BF16)),
        in_specs=[vmem] * 5,
        out_specs=(hbm, hbm),
        scratch_shapes=[
            held(*tiles, kind=F32),
            held(*tiles),
            pltpu.SemaphoreType.DMA((2,)),
        ],
        compiler_params=pltpu.CompilerParams(vmem_limit_bytes=16 << 20),
    )(result, grads, back, held_mix, done)
    return unpacked(result, rows, width, chans), unpacked(field_grad, rows, width, chans)


def solution(mesh):
    return jax.shard_map(
        on_device,
        mesh=mesh,
        in_specs=(
            P("lat", "lon", None),
            P(),
            P(None, "lat", None, None),
            P("lat"),
            P(),
            P(),
            P("lat", "lon", None),
        ),
        out_specs=(P("lat", "lon", None), P("lat", "lon", None)),
        check_vma=False,
    )
```

```python
import functools

import jax
import jax.numpy as jnp
from jax import lax
from jax.experimental import pallas as pl
from jax.experimental.pallas import tpu as pltpu
from jax.sharding import PartitionSpec as P

KB = 4
REACH = 8
TAPS = 2 * REACH + 1
WIDE = 2 * REACH
CH = 256
HID = 512
ROWS = 4
LANES = 128
RING = 128
CELLS = 112
OUTC = 96
MESH = pl.DeviceIdType.MESH
F32 = jnp.float32
BF16 = jnp.bfloat16


def dot(left, right):
    return jnp.dot(left, right, preferred_element_type=F32)


def dot_last(left, right):
    return lax.dot_general(left, right, (((1,), (1,)), ((), ())), preferred_element_type=F32)


def circulant(taps, count, start):
    spread = jnp.broadcast_to(taps, (count, RING))
    return pltpu.roll(spread, (start - REACH) % RING, 1, stride=1, stride_axis=0)


def packed(grid):
    rows, width, chans = grid.shape
    tiles = grid.transpose(1, 0, 2).reshape(width, rows, chans // LANES, LANES)
    return tiles.transpose(0, 2, 1, 3).reshape(width * rows * chans // LANES, LANES)


def unpacked(tiles, rows, width, chans):
    grid = tiles.reshape(width, chans // LANES, rows, LANES).transpose(0, 2, 1, 3)
    return grid.reshape(width, rows, chans).transpose(1, 0, 2)


def read_row(tiles, row, width):
    return jnp.concatenate(
        [tiles[pl.ds(half * ROWS + row, width, stride=2 * ROWS), :] for half in range(2)], axis=1
    )


def write_row(tiles, row, width, value):
    for half in range(2):
        tiles[pl.ds(half * ROWS + row, width, stride=2 * ROWS), :] = value[
            :, half * LANES : (half + 1) * LANES
        ]


def place():
    lat, lon = lax.axis_index("lat"), lax.axis_index("lon")
    lats, lons = lax.axis_size("lat"), lax.axis_size("lon")
    odd = lax.rem(lat, 2)
    near = jnp.where(odd == 1, lat - 1, lat + 1)
    far = jnp.where(odd == 1, lat + 1, lat - 1)
    has_far = jnp.logical_and(far >= 0, far < lats)
    west = lax.rem(lon + lons - 1, lons)
    east = lax.rem(lon + 1, lons)
    return lat, lon, odd, near, far, has_far, west, east


def owned(odd, row):
    return jnp.where(odd == 1, row, ROWS - 1 - row)


def forward_kernel(
    width,
    fields_hbm, cot_hbm, w_mix_hbm, w_up_hbm, w_down_hbm, filters_hbm, reach_hbm,
    result_ref, grads_ref, back_ref, w_mix, done_ref,
    raw, raw_cot, wide, filters_ref, filters_wide, reach_ref,
    own, edge, cot_w, cot_e, taps_own, near_in, far_in, taps_near, taps_far,
    w_in, e_in, cw_in, ce_in, nw_in, ne_in, ncw_in, nce_in, fw_in, fe_in, fcw_in, fce_in,
    cells, cots, taps, taps_rev, fwd, partial_ref, w_up, w_down,
    load_sem, send_sem, recv_sem, told,
):
    lat, lon, odd, near, far, has_far, west, east = place()

    barrier = pltpu.get_barrier_semaphore()
    lons = lax.axis_size("lon")
    even = odd == 0
    upper = lax.rem(lat, 4) >= 2
    even_lat = lat - odd
    desk = even_lat + 1
    far_even = far - lax.rem(far, 2)
    origin = jnp.logical_and(lat == 0, lon == 0)
    origin_mate = jnp.logical_and(lat == 1, lon == 0)
    beside = jnp.logical_or(lon == 1, lon == lons - 1)
    beside_desk = jnp.logical_and(lat == 1, beside)
    beside_even = jnp.logical_and(lat == 0, beside)
    mate = (near, lon)
    root = (0, 0)

    def both(left, right):
        return jnp.logical_and(left, right)

    def no(flag):
        return jnp.logical_not(flag)

    def greet(target):
        pl.semaphore_signal(barrier, inc=1, device_id=target, device_id_type=MESH)

    def tell(index):
        pl.semaphore_signal(told.at[index], inc=1, device_id=mate, device_id_type=MESH)

    @pl.when(both(no(origin), no(origin_mate)))
    def _():
        greet(mate)

    @pl.when(no(origin))
    def _():
        greet((desk, west))
        greet((desk, east))

    @pl.when(has_far)
    def _():
        for target in ((far_even, lon), (far_even, west), (far_even, east)):
            greet(target)

    fars = jnp.where(even_lat > 0, 1, 0) + jnp.where(desk < lax.axis_size("lat") - 1, 1, 0)
    even_count = 1 + 3 * fars + jnp.where(origin, 2, 0)
    odd_count = 5 - jnp.where(jnp.logical_or(origin_mate, beside_desk), 1, 0)

    loads = [
        (fields_hbm, raw), (cot_hbm, raw_cot), (filters_hbm, filters_ref), (reach_hbm, reach_ref),
        (w_mix_hbm, w_mix), (w_up_hbm, w_up), (w_down_hbm, w_down),
    ]
    loads = [pltpu.make_async_copy(s, d, load_sem.at[i]) for i, (s, d) in enumerate(loads)]
    for load in loads:
        load.start()

    for load, source, slots in ((loads[0], raw, (1, 2, 3, 4)), (loads[1], raw_cot, (0, 6, 7, 5))):
        load.wait()
        wide[0 : source.shape[0]] = source[...].astype(F32)
        for row in range(ROWS):
            own[slots[row]] = read_row(wide, owned(odd, row), width).astype(BF16)

    loads[2].wait()
    loads[3].wait()
    taps[...] = jnp.zeros_like(taps)
    filters_wide[0 : 3 * KB * ROWS] = filters_ref[...].astype(F32)
    lane = lax.broadcasted_iota(jnp.int32, (1, TAPS), 1) - REACH
    for row in range(ROWS):
        keep = jnp.abs(lane) <= reach_ref[owned(odd, row)]
        lines = filters_wide[pl.ds(owned(odd, row), 3 * KB, stride=ROWS), :]
        taps[1 + row, 0 : 3 * KB, 0:TAPS] = jnp.where(keep, lines, 0.0)
    taps_own[0] = taps[1].astype(BF16)
    taps_own[1] = taps[ROWS].astype(BF16)

    edge[...] = own[1:5, width - WIDE : width]
    for row, slot in enumerate((0, 6, 7, 5)):
        cot_w[row] = own[slot, 0:REACH]
        cot_e[row] = own[slot, width - REACH : width]

    def remote(index, source, target, device, arrive=None):
        return pltpu.make_async_remote_copy(
            src_ref=source, dst_ref=target, send_sem=send_sem.at[index],
            recv_sem=recv_sem.at[index if arrive is None else arrive], device_id=device, device_id_type=MESH,
        )

    head = pl.ds(0, WIDE)
    far_sends = [
        remote(0, taps_own.at[1], taps_far, (far, lon)),
        remote(1, own.at[pl.ds(3, 2)], far_in.at[pl.ds(0, 2)], (far, lon)),
        remote(2, own.at[pl.ds(3, 2), head], fe_in, (far, west)),
        remote(3, cot_w.at[3], fce_in, (far, west)),
        remote(4, edge.at[pl.ds(2, 2)], fw_in, (far, east)),
        remote(5, cot_e.at[3], fcw_in, (far, east)),
        remote(16, own.at[5], far_in.at[2], (far, lon)),
    ]
    west_sends = [
        remote(6, own.at[pl.ds(1, 4), head], e_in, (lat, west)),
        remote(7, cot_w, ce_in, (lat, west)),
    ]
    east_sends = [
        remote(8, edge, w_in, (lat, east)),
        remote(9, cot_e, cw_in, (lat, east)),
    ]
    mate_sends = [
        remote(10, taps_own.at[0], taps_near, mate),
        remote(11, own.at[pl.ds(0, 3)], near_in, mate),
    ]
    corner_sends = [
        remote(12, e_in.at[pl.ds(0, 2)], ne_in, mate),
        remote(13, ce_in.at[0], nce_in, mate),
        remote(14, w_in.at[pl.ds(0, 2)], nw_in, mate),
        remote(15, cw_in.at[0], ncw_in, mate),
    ]
    corner_west_sends = [
        remote(17, own.at[pl.ds(1, 2), head], ne_in, (near, west), 12),
        remote(18, cot_w.at[0], nce_in, (near, west), 13),
    ]
    corner_east_sends = [
        remote(19, edge.at[pl.ds(0, 2)], nw_in, (near, east), 14),
        remote(20, cot_e.at[0], ncw_in, (near, east), 15),
    ]
    corner_west = both(beside_even, lon == 1)
    corner_east = both(beside_even, lon == lons - 1)
    groups = (west_sends, east_sends, mate_sends)
    lon_sends = west_sends + east_sends
    near_sends = mate_sends + corner_sends

    def start(copies):
        for copy in copies:
            copy.start()

    def start_sides():
        west_last, east_last = lon == 1, lon == lons - 1
        pl.when(no(both(beside_even, west_last)))(functools.partial(start, west_sends))
        pl.when(no(both(beside_even, east_last)))(functools.partial(start, east_sends))
        pl.when(corner_west)(functools.partial(start, corner_west_sends))
        pl.when(corner_east)(functools.partial(start, corner_east_sends))

    @pl.when(origin)
    def _():
        pl.semaphore_wait(barrier, even_count)
        for target in ((1, 0), (1, 1), (1, lons - 1)):
            greet(target)

    @pl.when(jnp.logical_and(upper, even))
    def _():
        pl.semaphore_wait(barrier, even_count)
        tell(0)

    @pl.when(jnp.logical_and(no(upper), no(even)))
    def _():
        pl.semaphore_wait(barrier, odd_count)
        pl.when(jnp.logical_or(origin_mate, beside_desk))(functools.partial(greet, root))
        pl.when(no(origin_mate))(functools.partial(tell, 0))

    @pl.when(upper == (odd == 1))
    def _():
        pl.semaphore_wait(told.at[0], 1)

    pl.when(both(upper, has_far))(functools.partial(start, far_sends[2:6] + far_sends[:1]))
    pl.when(no(upper))(start_sides)
    pl.when(no(origin_mate))(functools.partial(start, mate_sends))

    @pl.when(origin_mate)
    def _():
        pl.semaphore_wait(barrier, 1)
        tell(0)
        start(mate_sends)

    @pl.when(jnp.logical_not(has_far))
    def _():
        for ref in (far_in, taps_far, fe_in, fce_in, fw_in, fcw_in):
            ref[...] = jnp.zeros_like(ref)

    first = lax.broadcasted_iota(jnp.int32, (RING, RING), 0)
    second = lax.broadcasted_iota(jnp.int32, (RING, RING), 1)
    flip = (first + second == 2 * REACH).astype(BF16)

    def tap_line(tap, basis):
        return basis * 3 + jnp.where(odd == 1, tap, 2 - tap)

    def reverse(row):
        taps_rev[row + 1] = dot(taps[row + 1].astype(BF16), flip)

    def forward_matrix(row):
        for tap in range(3):
            for basis in range(KB):
                line = taps[row + 1, pl.ds(tap_line(tap, basis), 1), :]
                block = jnp.concatenate(
                    [circulant(line, 104, 0), circulant(line, REACH, RING - REACH)], axis=0
                )
                fwd[row + 1, basis * CELLS : (basis + 1) * CELLS, tap * RING : (tap + 1) * RING] = (
                    block.astype(BF16)
                )

    def backward_blocks(source):
        for out in range(max(0, source - 1), min(ROWS, source + 2)):
            tap, slot = out - source + 1, source - out + 1
            for basis in range(KB):
                line = taps_rev[source + 1, pl.ds(tap_line(tap, basis), 1), :]
                back_ref[out, basis * OUTC : (basis + 1) * OUTC, slot * RING : (slot + 1) * RING] = (
                    circulant(line, OUTC, 0).astype(BF16)
                )

    @pl.when(both(no(upper), even))
    def _():
        pl.when(no(origin))(lambda: pl.semaphore_wait(barrier, even_count))
        tell(1)

    @pl.when(both(upper, no(even)))
    def _():
        pl.semaphore_wait(barrier, odd_count)
        tell(1)

    @pl.when(upper == even)
    def _():
        pl.semaphore_wait(told.at[1], 1)

    pl.when(both(no(upper), has_far))(
        functools.partial(start, far_sends[2:6] + far_sends[:2] + far_sends[6:])
    )

    pl.when(upper)(start_sides)
    pl.when(both(upper, has_far))(functools.partial(start, far_sends[1:2] + far_sends[6:]))

    @pl.when(beside_desk)
    def _():
        pl.semaphore_wait(barrier, 1)
        tell(2)

    @pl.when(beside_even)
    def _():
        pl.semaphore_wait(told.at[2], 1)
        pl.when(lon == 1)(functools.partial(start, west_sends))
        pl.when(lon == lons - 1)(functools.partial(start, east_sends))

    for row in range(ROWS):
        reverse(row)
        forward_matrix(row)
        backward_blocks(row)

    for load in loads[4:]:
        load.wait()

    def fill_cells(row, middle, west_part, east_part):
        cells[row + 2, 0:width] = middle
        cells[row + 2, width : width + WIDE] = east_part
        cells[row + 2, width + WIDE : RING - WIDE] = jnp.zeros(
            (RING - 2 * WIDE - width, CH), BF16
        )
        cells[row + 2, RING - WIDE : RING] = west_part

    def fill_cots(row, middle, west_part, east_part):
        cots[row + 1, 0:width] = middle
        cots[row + 1, width : width + REACH] = east_part
        cots[row + 1, width + REACH : 104] = jnp.zeros((104 - REACH - width, CH), BF16)
        cots[row + 1, 104:CELLS] = west_part

    def conv_part(row, begin, end):
        source = cells[row + 1 + begin : row + 1 + end].reshape((end - begin) * RING, CH)
        return dot(fwd[row + 1, :, begin * RING : end * RING], source)

    def advance(rows, ready=None, between=None):
        count = len(rows)
        convs = []
        for n, row in enumerate(rows):
            if ready is None:
                conv = conv_part(row, 0, 3)
            else:
                conv = partial_ref[n] + conv_part(row, ready[n], 3)
            convs.append(conv.astype(BF16))
        spatial = jnp.zeros((count * CELLS, CH), F32)
        for basis in range(KB):
            part = jnp.concatenate(
                [c[basis * CELLS : (basis + 1) * CELLS] for c in convs], axis=0
            )
            spatial = spatial + dot(part, w_mix[:, basis * CH : (basis + 1) * CH])
        centre = jnp.concatenate(
            [p for row in rows for p in (cells[row + 2, 0:104].astype(F32), cells[row + 2, 120:128].astype(F32))],
            axis=0,
        )
        hidden = (centre + spatial).astype(BF16)
        pre = dot(hidden, w_up[...])
        half = 0.5 * (1.0 + lax.erf(pre * 0.7071067811865476))
        slope = half + pre * jnp.exp(-0.5 * pre * pre) * 0.3989422804014327
        active = (half * pre).astype(BF16)
        for n, row in enumerate(rows):
            base = n * CELLS
            if 0 <= row < ROWS:
                result = hidden[base : base + OUTC].astype(F32) + dot(
                    active[base : base + OUTC], w_down[...]
                )
                write_row(wide, owned(odd, row), width, result[:width])
        if between is not None:
            between()
        upstream = jnp.concatenate([cots[row + 1] for row in rows], axis=0)
        grad_active = (dot_last(upstream, w_down[...]) * slope).astype(BF16)
        grad = (upstream.astype(F32) + dot_last(grad_active, w_up[...])).astype(BF16)
        for n, row in enumerate(rows):
            base = n * CELLS
            grads_ref[row + 1, 0:104] = grad[base : base + 104]
            grads_ref[row + 1, 104:120] = jnp.zeros((WIDE, CH), BF16)
            grads_ref[row + 1, 120:128] = grad[base + 104 : base + CELLS]

    def finish(rows):
        return retreat(rows, grads_ref, back_ref, w_mix)

    for copy in lon_sends:
        copy.wait_recv()
    pl.when(no(origin))(functools.partial(start, corner_sends))
    for row in range(ROWS):
        fill_cells(row, own[1 + row], w_in[row], e_in[row])
        fill_cots(row, own[(0, 6, 7, 5)[row]], cw_in[row], ce_in[row])
    advance((1, 2))

    mate_sends[0].wait_recv()
    taps[0] = taps_near[...].astype(F32)
    reverse(-1)
    forward_matrix(-1)
    backward_blocks(-1)
    for copy in near_sends[1:]:
        copy.wait_recv()
    fill_cells(-1, near_in[1], nw_in[0], ne_in[0])
    fill_cells(-2, near_in[2], nw_in[1], ne_in[1])
    fill_cots(-1, near_in[0], ncw_in[...], nce_in[...])
    advance((0, -1))
    done_ref[...] = finish((0, 1))

    pl.when(has_far)(far_sends[0].wait_recv)
    taps[ROWS + 1] = taps_far[...].astype(F32)
    reverse(ROWS)
    forward_matrix(ROWS)
    backward_blocks(ROWS)
    partial_ref[0] = conv_part(ROWS - 1, 0, 2)
    partial_ref[1] = conv_part(ROWS, 0, 1)

    @pl.when(has_far)
    def _():
        for copy in far_sends[1:6]:
            copy.wait_recv()

    fill_cells(ROWS, far_in[1], fw_in[1], fe_in[1])
    fill_cells(ROWS + 1, far_in[0], fw_in[0], fe_in[0])

    def last_cots():
        result_ref[...] = wide[0 : result_ref.shape[0]].astype(BF16)
        pl.when(has_far)(far_sends[6].wait_recv)
        fill_cots(ROWS, far_in[2], fcw_in[...], fce_in[...])

    advance((ROWS - 1, ROWS), ready=(2, 1), between=last_cots)

    def drain(copies):
        for copy in copies:
            copy.wait_send()

    for copies in groups:
        drain(copies)
    pl.when(no(origin))(functools.partial(drain, corner_sends))
    pl.when(corner_west)(functools.partial(drain, corner_west_sends))
    pl.when(corner_east)(functools.partial(drain, corner_east_sends))

    @pl.when(has_far)
    def _():
        for copy in far_sends:
            copy.wait_send()


def retreat(rows, grads_ref, back_ref, w_mix):
    convs = []
    for row in rows:
        source = grads_ref[row : row + 3].reshape(3 * RING, CH)
        convs.append(dot(back_ref[row], source).astype(BF16))
    total = jnp.concatenate([grads_ref[row + 1, 0:OUTC].astype(F32) for row in rows], axis=0)
    for basis in range(KB):
        part = jnp.concatenate([c[basis * OUTC : (basis + 1) * OUTC] for c in convs], axis=0)
        total = total + dot_last(part, w_mix[:, basis * CH : (basis + 1) * CH])
    return total


def backward_kernel(
    width, packed_result, grads_ref, back_ref, w_mix, done_ref, result_hbm, grad_hbm, wide, out, sems
):
    odd = lax.rem(lax.axis_index("lat"), 2)
    store_result = pltpu.make_async_copy(packed_result, result_hbm, sems.at[0])
    store_result.start()
    total = retreat((2, 3), grads_ref, back_ref, w_mix)
    for row in (0, 1):
        write_row(wide, owned(odd, row), width, done_ref[row * OUTC : row * OUTC + width])
        write_row(wide, owned(odd, 2 + row), width, total[row * OUTC : row * OUTC + width])
    out[...] = wide[0 : out.shape[0]].astype(BF16)
    store_grad = pltpu.make_async_copy(out, grad_hbm, sems.at[1])
    store_grad.start()
    store_result.wait()
    store_grad.wait()


def on_device(fields, w_mix, filters, reach, w_up, w_down, cotangent):
    rows, width, chans = fields.shape
    hbm = pl.BlockSpec(memory_space=pltpu.HBM)
    vmem = pl.BlockSpec(memory_space=pltpu.VMEM)
    tiles = (width * rows * chans // LANES, LANES)
    roomy = (-(-width // 8) * 8 * rows * chans // LANES, LANES)

    def held(*shape, kind=BF16):
        return pltpu.VMEM(shape, kind)

    sources = (
        packed(fields), packed(cotangent), w_mix, w_up, w_down,
        filters.transpose(0, 2, 1, 3).reshape(3 * KB * rows, TAPS), reach,
    )
    sources = [pltpu.with_memory_space_constraint(source, pltpu.HBM) for source in sources]
    result, grads, back, held_mix, done = pl.pallas_call(
        functools.partial(forward_kernel, width),
        name="halo_forward",
        out_shape=(
            held(*tiles),
            held(rows + 2, RING, chans),
            held(rows, KB * OUTC, 3 * RING),
            held(chans, KB * chans),
            held(2 * OUTC, chans, kind=F32),
        ),
        in_specs=[hbm] * 7,
        out_specs=(vmem,) * 5,
        scratch_shapes=[
            held(*tiles),
            held(*tiles),
            held(*roomy, kind=F32),
            held(3 * KB * rows, TAPS),
            held(4 * KB * rows, TAPS, kind=F32),
            pltpu.SMEM((rows,), jnp.int32),
            held(8, width, chans),
            held(rows, WIDE, chans),
            held(rows, REACH, chans),
            held(rows, REACH, chans),
            held(2, 16, RING),
            held(3, width, chans),
            held(3, width, chans),
            held(16, RING),
            held(16, RING),
            held(rows, WIDE, chans),
            held(rows, WIDE, chans),
            held(rows, REACH, chans),
            held(rows, REACH, chans),
            held(2, WIDE, chans),
            held(2, WIDE, chans),
            held(REACH, chans),
            held(REACH, chans),
            held(2, WIDE, chans),
            held(2, WIDE, chans),
            held(REACH, chans),
            held(REACH, chans),
            held(rows + 4, RING, chans),
            held(rows + 2, CELLS, chans),
            held(rows + 2, 16, RING, kind=F32),
            held(rows + 2, 16, RING, kind=F32),
            held(rows + 2, KB * CELLS, 3 * RING),
            held(2, KB * CELLS, chans, kind=F32),
            held(chans, HID),
            held(HID, chans),
            pltpu.SemaphoreType.DMA((7,)),
            pltpu.SemaphoreType.DMA((21,)),
            pltpu.SemaphoreType.DMA((17,)),
            pltpu.SemaphoreType.REGULAR((3,)),
        ],
        compiler_params=pltpu.CompilerParams(
            collective_id=0, has_side_effects=True, vmem_limit_bytes=24 << 20
        ),
    )(*sources)
    result, field_grad = pl.pallas_call(
        functools.partial(backward_kernel, width),
        name="transposed_mix",
        out_shape=(pltpu.HBM(tiles, BF16), pltpu.HBM(tiles, BF16)),
        in_specs=[vmem] * 5,
        out_specs=(hbm, hbm),
        scratch_shapes=[
            held(*roomy, kind=F32),
            held(*tiles),
            pltpu.SemaphoreType.DMA((2,)),
        ],
        compiler_params=pltpu.CompilerParams(vmem_limit_bytes=16 << 20),
    )(result, grads, back, held_mix, done)
    return unpacked(result, rows, width, chans), unpacked(field_grad, rows, width, chans)


def solution(mesh):
    return jax.shard_map(
        on_device,
        mesh=mesh,
        in_specs=(
            P("lat", "lon", None),
            P(),
            P(None, "lat", None, None),
            P("lat"),
            P(),
            P(),
            P("lat", "lon", None),
        ),
        out_specs=(P("lat", "lon", None), P("lat", "lon", None)),
        check_vma=False,
    )
```

```python
import functools

import jax
import jax.numpy as jnp
from jax import lax
from jax.experimental import pallas as pl
from jax.experimental.pallas import tpu as pltpu
from jax.sharding import PartitionSpec as P

KB = 4
REACH = 8
TAPS = 2 * REACH + 1
WIDE = 2 * REACH
CH = 256
HID = 512
ROWS = 4
LANES = 128
RING = 128
CELLS = 112
OUTC = 96
MESH = pl.DeviceIdType.MESH
F32 = jnp.float32
BF16 = jnp.bfloat16


def dot(left, right):
    return jnp.dot(left, right, preferred_element_type=F32)


def dot_last(left, right):
    return lax.dot_general(left, right, (((1,), (1,)), ((), ())), preferred_element_type=F32)


def circulant(taps, count, start):
    spread = jnp.broadcast_to(taps, (count, RING))
    return pltpu.roll(spread, (start - REACH) % RING, 1, stride=1, stride_axis=0)


def packed(grid):
    rows, width, chans = grid.shape
    tiles = grid.transpose(1, 0, 2).reshape(width, rows, chans // LANES, LANES)
    return tiles.transpose(0, 2, 1, 3).reshape(width * rows * chans // LANES, LANES)


def unpacked(tiles, rows, width, chans):
    grid = tiles.reshape(width, chans // LANES, rows, LANES).transpose(0, 2, 1, 3)
    return grid.reshape(width, rows, chans).transpose(1, 0, 2)


def read_row(tiles, row, width):
    return jnp.concatenate(
        [tiles[pl.ds(half * ROWS + row, width, stride=2 * ROWS), :] for half in range(2)], axis=1
    )


def write_row(tiles, row, width, value):
    for half in range(2):
        tiles[pl.ds(half * ROWS + row, width, stride=2 * ROWS), :] = value[
            :, half * LANES : (half + 1) * LANES
        ]


def place():
    lat, lon = lax.axis_index("lat"), lax.axis_index("lon")
    lats, lons = lax.axis_size("lat"), lax.axis_size("lon")
    odd = lax.rem(lat, 2)
    near = jnp.where(odd == 1, lat - 1, lat + 1)
    far = jnp.where(odd == 1, lat + 1, lat - 1)
    has_far = jnp.logical_and(far >= 0, far < lats)
    west = lax.rem(lon + lons - 1, lons)
    east = lax.rem(lon + 1, lons)
    return lat, lon, odd, near, far, has_far, west, east


def owned(odd, row):
    return jnp.where(odd == 1, row, ROWS - 1 - row)


def forward_kernel(
    width,
    fields_hbm, cot_hbm, w_mix_hbm, w_up_hbm, w_down_hbm, filters_hbm, reach_hbm,
    result_ref, grads_ref, back_ref, w_mix, done_ref, begun_ref,
    raw, raw_cot, wide, filters_ref, filters_wide, reach_ref,
    own, edge, cot_w, cot_e, taps_own, near_in, far_in, taps_near, taps_far,
    w_in, e_in, cw_in, ce_in, nw_in, ne_in, ncw_in, nce_in, fw_in, fe_in, fcw_in, fce_in,
    cells, cots, taps, taps_rev, fwd, partial_ref, w_up, w_down,
    load_sem, send_sem, recv_sem, told,
):
    lat, lon, odd, near, far, has_far, west, east = place()

    barrier = pltpu.get_barrier_semaphore()
    lons = lax.axis_size("lon")
    even = odd == 0
    upper = lax.rem(lat, 4) >= 2
    even_lat = lat - odd
    desk = even_lat + 1
    far_even = far - lax.rem(far, 2)
    origin = jnp.logical_and(lat == 0, lon == 0)
    origin_mate = jnp.logical_and(lat == 1, lon == 0)
    beside = jnp.logical_or(lon == 1, lon == lons - 1)
    beside_desk = jnp.logical_and(lat == 1, beside)
    beside_even = jnp.logical_and(lat == 0, beside)
    mate = (near, lon)
    root = (0, 0)

    def both(left, right):
        return jnp.logical_and(left, right)

    def no(flag):
        return jnp.logical_not(flag)

    def greet(target):
        pl.semaphore_signal(barrier, inc=1, device_id=target, device_id_type=MESH)

    def tell(index):
        pl.semaphore_signal(told.at[index], inc=1, device_id=mate, device_id_type=MESH)

    @pl.when(both(no(origin), no(origin_mate)))
    def _():
        greet(mate)

    @pl.when(no(origin))
    def _():
        greet((desk, west))
        greet((desk, east))

    @pl.when(has_far)
    def _():
        for target in ((far_even, lon), (far_even, west), (far_even, east)):
            greet(target)

    fars = jnp.where(even_lat > 0, 1, 0) + jnp.where(desk < lax.axis_size("lat") - 1, 1, 0)
    even_count = 1 + 3 * fars + jnp.where(origin, 2, 0)
    odd_count = 5 - jnp.where(jnp.logical_or(origin_mate, beside_desk), 1, 0)

    loads = [
        (fields_hbm, raw), (cot_hbm, raw_cot), (filters_hbm, filters_ref), (reach_hbm, reach_ref),
        (w_mix_hbm, w_mix), (w_up_hbm, w_up), (w_down_hbm, w_down),
    ]
    loads = [pltpu.make_async_copy(s, d, load_sem.at[i]) for i, (s, d) in enumerate(loads)]
    for load in loads:
        load.start()

    for load, source, slots in ((loads[0], raw, (1, 2, 3, 4)), (loads[1], raw_cot, (0, 6, 7, 5))):
        load.wait()
        wide[0 : source.shape[0]] = source[...].astype(F32)
        for row in range(ROWS):
            own[slots[row]] = read_row(wide, owned(odd, row), width).astype(BF16)

    loads[2].wait()
    loads[3].wait()
    taps[...] = jnp.zeros_like(taps)
    filters_wide[0 : 3 * KB * ROWS] = filters_ref[...].astype(F32)
    lane = lax.broadcasted_iota(jnp.int32, (1, TAPS), 1) - REACH
    for row in range(ROWS):
        keep = jnp.abs(lane) <= reach_ref[owned(odd, row)]
        lines = filters_wide[pl.ds(owned(odd, row), 3 * KB, stride=ROWS), :]
        taps[1 + row, 0 : 3 * KB, 0:TAPS] = jnp.where(keep, lines, 0.0)
    taps_own[0] = taps[1].astype(BF16)
    taps_own[1] = taps[ROWS].astype(BF16)

    edge[...] = own[1:5, width - WIDE : width]
    for row, slot in enumerate((0, 6, 7, 5)):
        cot_w[row] = own[slot, 0:REACH]
        cot_e[row] = own[slot, width - REACH : width]

    def remote(index, source, target, device, arrive=None):
        return pltpu.make_async_remote_copy(
            src_ref=source, dst_ref=target, send_sem=send_sem.at[index],
            recv_sem=recv_sem.at[index if arrive is None else arrive], device_id=device, device_id_type=MESH,
        )

    head = pl.ds(0, WIDE)
    far_sends = [
        remote(0, taps_own.at[1], taps_far, (far, lon)),
        remote(1, own.at[pl.ds(3, 2)], far_in.at[pl.ds(0, 2)], (far, lon)),
        remote(2, own.at[pl.ds(3, 2), head], fe_in, (far, west)),
        remote(3, cot_w.at[3], fce_in, (far, west)),
        remote(4, edge.at[pl.ds(2, 2)], fw_in, (far, east)),
        remote(5, cot_e.at[3], fcw_in, (far, east)),
        remote(16, own.at[5], far_in.at[2], (far, lon)),
    ]
    west_sends = [
        remote(6, own.at[pl.ds(1, 4), head], e_in, (lat, west)),
        remote(7, cot_w, ce_in, (lat, west)),
    ]
    east_sends = [
        remote(8, edge, w_in, (lat, east)),
        remote(9, cot_e, cw_in, (lat, east)),
    ]
    mate_sends = [
        remote(10, taps_own.at[0], taps_near, mate),
        remote(11, own.at[pl.ds(0, 3)], near_in, mate),
    ]
    corner_sends = [
        remote(12, e_in.at[pl.ds(0, 2)], ne_in, mate),
        remote(13, ce_in.at[0], nce_in, mate),
        remote(14, w_in.at[pl.ds(0, 2)], nw_in, mate),
        remote(15, cw_in.at[0], ncw_in, mate),
    ]
    corner_west_sends = [
        remote(17, own.at[pl.ds(1, 2), head], ne_in, (near, west), 12),
        remote(18, cot_w.at[0], nce_in, (near, west), 13),
    ]
    corner_east_sends = [
        remote(19, edge.at[pl.ds(0, 2)], nw_in, (near, east), 14),
        remote(20, cot_e.at[0], ncw_in, (near, east), 15),
    ]
    corner_west = both(beside_even, lon == 1)
    corner_east = both(beside_even, lon == lons - 1)
    groups = (west_sends, east_sends, mate_sends)
    lon_sends = west_sends + east_sends
    near_sends = mate_sends + corner_sends

    def start(copies):
        for copy in copies:
            copy.start()

    def start_sides():
        west_last, east_last = lon == 1, lon == lons - 1
        pl.when(no(both(beside_even, west_last)))(functools.partial(start, west_sends))
        pl.when(no(both(beside_even, east_last)))(functools.partial(start, east_sends))
        pl.when(corner_west)(functools.partial(start, corner_west_sends))
        pl.when(corner_east)(functools.partial(start, corner_east_sends))

    @pl.when(origin)
    def _():
        pl.semaphore_wait(barrier, even_count)
        for target in ((1, 0), (1, 1), (1, lons - 1)):
            greet(target)

    @pl.when(jnp.logical_and(upper, even))
    def _():
        pl.semaphore_wait(barrier, even_count)
        tell(0)

    @pl.when(jnp.logical_and(no(upper), no(even)))
    def _():
        pl.semaphore_wait(barrier, odd_count)
        pl.when(jnp.logical_or(origin_mate, beside_desk))(functools.partial(greet, root))
        pl.when(no(origin_mate))(functools.partial(tell, 0))

    @pl.when(upper == (odd == 1))
    def _():
        pl.semaphore_wait(told.at[0], 1)

    pl.when(both(upper, has_far))(functools.partial(start, far_sends[2:6] + far_sends[:1]))
    pl.when(no(upper))(start_sides)
    pl.when(no(origin_mate))(functools.partial(start, mate_sends))

    @pl.when(origin_mate)
    def _():
        pl.semaphore_wait(barrier, 1)
        tell(0)
        start(mate_sends)

    @pl.when(jnp.logical_not(has_far))
    def _():
        for ref in (far_in, taps_far, fe_in, fce_in, fw_in, fcw_in):
            ref[...] = jnp.zeros_like(ref)

    first = lax.broadcasted_iota(jnp.int32, (RING, RING), 0)
    second = lax.broadcasted_iota(jnp.int32, (RING, RING), 1)
    flip = (first + second == 2 * REACH).astype(BF16)

    def tap_line(tap, basis):
        return basis * 3 + jnp.where(odd == 1, tap, 2 - tap)

    def reverse(row):
        taps_rev[row + 1] = dot(taps[row + 1].astype(BF16), flip)

    def forward_matrix(row):
        for tap in range(3):
            for basis in range(KB):
                line = taps[row + 1, pl.ds(tap_line(tap, basis), 1), :]
                block = jnp.concatenate(
                    [circulant(line, 104, 0), circulant(line, REACH, RING - REACH)], axis=0
                )
                fwd[row + 1, basis * CELLS : (basis + 1) * CELLS, tap * RING : (tap + 1) * RING] = (
                    block.astype(BF16)
                )

    def backward_blocks(source):
        for out in range(max(0, source - 1), min(ROWS, source + 2)):
            tap, slot = out - source + 1, source - out + 1
            for basis in range(KB):
                line = taps_rev[source + 1, pl.ds(tap_line(tap, basis), 1), :]
                back_ref[out, basis * OUTC : (basis + 1) * OUTC, slot * RING : (slot + 1) * RING] = (
                    circulant(line, OUTC, 0).astype(BF16)
                )

    @pl.when(both(no(upper), even))
    def _():
        pl.when(no(origin))(lambda: pl.semaphore_wait(barrier, even_count))
        tell(1)

    @pl.when(both(upper, no(even)))
    def _():
        pl.semaphore_wait(barrier, odd_count)
        tell(1)

    @pl.when(upper == even)
    def _():
        pl.semaphore_wait(told.at[1], 1)

    pl.when(both(no(upper), has_far))(
        functools.partial(start, far_sends[2:6] + far_sends[:2] + far_sends[6:])
    )

    pl.when(upper)(start_sides)
    pl.when(both(upper, has_far))(functools.partial(start, far_sends[1:2] + far_sends[6:]))

    @pl.when(beside_desk)
    def _():
        pl.semaphore_wait(barrier, 1)
        tell(2)

    @pl.when(beside_even)
    def _():
        pl.semaphore_wait(told.at[2], 1)
        pl.when(lon == 1)(functools.partial(start, west_sends))
        pl.when(lon == lons - 1)(functools.partial(start, east_sends))

    for row in range(ROWS):
        reverse(row)
        forward_matrix(row)
        backward_blocks(row)

    for load in loads[4:]:
        load.wait()

    def fill_cells(row, middle, west_part, east_part):
        cells[row + 2, 0:width] = middle
        cells[row + 2, width : width + WIDE] = east_part
        cells[row + 2, width + WIDE : RING - WIDE] = jnp.zeros(
            (RING - 2 * WIDE - width, CH), BF16
        )
        cells[row + 2, RING - WIDE : RING] = west_part

    def fill_cots(row, middle, west_part, east_part):
        cots[row + 1, 0:width] = middle
        cots[row + 1, width : width + REACH] = east_part
        cots[row + 1, width + REACH : 104] = jnp.zeros((104 - REACH - width, CH), BF16)
        cots[row + 1, 104:CELLS] = west_part

    def conv_part(row, begin, end):
        source = cells[row + 1 + begin : row + 1 + end].reshape((end - begin) * RING, CH)
        return dot(fwd[row + 1, :, begin * RING : end * RING], source)

    def advance(rows, ready=None, between=None):
        count = len(rows)
        convs = []
        for n, row in enumerate(rows):
            if ready is None:
                conv = conv_part(row, 0, 3)
            else:
                conv = partial_ref[n] + conv_part(row, ready[n], 3)
            convs.append(conv.astype(BF16))
        spatial = jnp.zeros((count * CELLS, CH), F32)
        for basis in range(KB):
            part = jnp.concatenate(
                [c[basis * CELLS : (basis + 1) * CELLS] for c in convs], axis=0
            )
            spatial = spatial + dot(part, w_mix[:, basis * CH : (basis + 1) * CH])
        centre = jnp.concatenate(
            [p for row in rows for p in (cells[row + 2, 0:104].astype(F32), cells[row + 2, 120:128].astype(F32))],
            axis=0,
        )
        hidden = (centre + spatial).astype(BF16)
        pre = dot(hidden, w_up[...])
        half = 0.5 * (1.0 + lax.erf(pre * 0.7071067811865476))
        slope = half + pre * jnp.exp(-0.5 * pre * pre) * 0.3989422804014327
        active = (half * pre).astype(BF16)
        for n, row in enumerate(rows):
            base = n * CELLS
            if 0 <= row < ROWS:
                result = hidden[base : base + OUTC].astype(F32) + dot(
                    active[base : base + OUTC], w_down[...]
                )
                write_row(wide, owned(odd, row), width, result[:width])
        if between is not None:
            between()
        upstream = jnp.concatenate([cots[row + 1] for row in rows], axis=0)
        grad_active = (dot_last(upstream, w_down[...]) * slope).astype(BF16)
        grad = (upstream.astype(F32) + dot_last(grad_active, w_up[...])).astype(BF16)
        for n, row in enumerate(rows):
            base = n * CELLS
            grads_ref[row + 1, 0:104] = grad[base : base + 104]
            grads_ref[row + 1, 104:120] = jnp.zeros((WIDE, CH), BF16)
            grads_ref[row + 1, 120:128] = grad[base + 104 : base + CELLS]

    def finish(rows):
        return retreat(rows, grads_ref, back_ref, w_mix)

    for copy in lon_sends:
        copy.wait_recv()
    pl.when(no(origin))(functools.partial(start, corner_sends))
    for row in range(ROWS):
        fill_cells(row, own[1 + row], w_in[row], e_in[row])
        fill_cots(row, own[(0, 6, 7, 5)[row]], cw_in[row], ce_in[row])
    advance((1, 2))

    mate_sends[0].wait_recv()
    taps[0] = taps_near[...].astype(F32)
    reverse(-1)
    forward_matrix(-1)
    backward_blocks(-1)
    for copy in near_sends[1:]:
        copy.wait_recv()
    fill_cells(-1, near_in[1], nw_in[0], ne_in[0])
    fill_cells(-2, near_in[2], nw_in[1], ne_in[1])
    fill_cots(-1, near_in[0], ncw_in[...], nce_in[...])
    advance((0, -1))
    done_ref[...] = finish((0, 1))

    pl.when(has_far)(far_sends[0].wait_recv)
    taps[ROWS + 1] = taps_far[...].astype(F32)
    reverse(ROWS)
    forward_matrix(ROWS)
    backward_blocks(ROWS)
    begun_ref[0] = back_part(2, 0, 2, grads_ref, back_ref)
    begun_ref[1] = back_part(3, 0, 1, grads_ref, back_ref)
    partial_ref[0] = conv_part(ROWS - 1, 0, 2)
    partial_ref[1] = conv_part(ROWS, 0, 1)

    @pl.when(has_far)
    def _():
        for copy in far_sends[1:6]:
            copy.wait_recv()

    fill_cells(ROWS, far_in[1], fw_in[1], fe_in[1])
    fill_cells(ROWS + 1, far_in[0], fw_in[0], fe_in[0])

    def last_cots():
        result_ref[...] = wide[0 : result_ref.shape[0]].astype(BF16)
        pl.when(has_far)(far_sends[6].wait_recv)
        fill_cots(ROWS, far_in[2], fcw_in[...], fce_in[...])

    advance((ROWS - 1, ROWS), ready=(2, 1), between=last_cots)

    def drain(copies):
        for copy in copies:
            copy.wait_send()

    for copies in groups:
        drain(copies)
    pl.when(no(origin))(functools.partial(drain, corner_sends))
    pl.when(corner_west)(functools.partial(drain, corner_west_sends))
    pl.when(corner_east)(functools.partial(drain, corner_east_sends))

    @pl.when(has_far)
    def _():
        for copy in far_sends:
            copy.wait_send()


def back_part(row, begin, end, grads_ref, back_ref):
    source = grads_ref[row + begin : row + end].reshape((end - begin) * RING, CH)
    return dot(back_ref[row, :, begin * RING : end * RING], source)


def retreat(rows, grads_ref, back_ref, w_mix, begun=None):
    convs = []
    for n, row in enumerate(rows):
        if begun is None:
            conv = back_part(row, 0, 3, grads_ref, back_ref)
        else:
            conv = begun[n] + back_part(row, 2 - n, 3, grads_ref, back_ref)
        convs.append(conv.astype(BF16))
    total = jnp.concatenate([grads_ref[row + 1, 0:OUTC].astype(F32) for row in rows], axis=0)
    for basis in range(KB):
        part = jnp.concatenate([c[basis * OUTC : (basis + 1) * OUTC] for c in convs], axis=0)
        total = total + dot_last(part, w_mix[:, basis * CH : (basis + 1) * CH])
    return total


def backward_kernel(
    width, packed_result, grads_ref, back_ref, w_mix, done_ref, begun_ref, result_hbm, grad_hbm, wide, out, sems
):
    odd = lax.rem(lax.axis_index("lat"), 2)
    store_result = pltpu.make_async_copy(packed_result, result_hbm, sems.at[0])
    store_result.start()
    total = retreat((2, 3), grads_ref, back_ref, w_mix, begun_ref)
    for row in (0, 1):
        write_row(wide, owned(odd, row), width, done_ref[row * OUTC : row * OUTC + width])
        write_row(wide, owned(odd, 2 + row), width, total[row * OUTC : row * OUTC + width])
    out[...] = wide[0 : out.shape[0]].astype(BF16)
    store_grad = pltpu.make_async_copy(out, grad_hbm, sems.at[1])
    store_grad.start()
    store_result.wait()
    store_grad.wait()


def on_device(fields, w_mix, filters, reach, w_up, w_down, cotangent):
    rows, width, chans = fields.shape
    hbm = pl.BlockSpec(memory_space=pltpu.HBM)
    vmem = pl.BlockSpec(memory_space=pltpu.VMEM)
    tiles = (width * rows * chans // LANES, LANES)
    roomy = (-(-width // 8) * 8 * rows * chans // LANES, LANES)

    def held(*shape, kind=BF16):
        return pltpu.VMEM(shape, kind)

    sources = (
        packed(fields), packed(cotangent), w_mix, w_up, w_down,
        filters.transpose(0, 2, 1, 3).reshape(3 * KB * rows, TAPS), reach,
    )
    sources = [pltpu.with_memory_space_constraint(source, pltpu.HBM) for source in sources]
    result, grads, back, held_mix, done, begun = pl.pallas_call(
        functools.partial(forward_kernel, width),
        name="halo_forward",
        out_shape=(
            held(*tiles),
            held(rows + 2, RING, chans),
            held(rows, KB * OUTC, 3 * RING),
            held(chans, KB * chans),
            held(2 * OUTC, chans, kind=F32),
            held(2, KB * OUTC, chans, kind=F32),
        ),
        in_specs=[hbm] * 7,
        out_specs=(vmem,) * 6,
        scratch_shapes=[
            held(*tiles),
            held(*tiles),
            held(*roomy, kind=F32),
            held(3 * KB * rows, TAPS),
            held(4 * KB * rows, TAPS, kind=F32),
            pltpu.SMEM((rows,), jnp.int32),
            held(8, width, chans),
            held(rows, WIDE, chans),
            held(rows, REACH, chans),
            held(rows, REACH, chans),
            held(2, 16, RING),
            held(3, width, chans),
            held(3, width, chans),
            held(16, RING),
            held(16, RING),
            held(rows, WIDE, chans),
            held(rows, WIDE, chans),
            held(rows, REACH, chans),
            held(rows, REACH, chans),
            held(2, WIDE, chans),
            held(2, WIDE, chans),
            held(REACH, chans),
            held(REACH, chans),
            held(2, WIDE, chans),
            held(2, WIDE, chans),
            held(REACH, chans),
            held(REACH, chans),
            held(rows + 4, RING, chans),
            held(rows + 2, CELLS, chans),
            held(rows + 2, 16, RING, kind=F32),
            held(rows + 2, 16, RING, kind=F32),
            held(rows + 2, KB * CELLS, 3 * RING),
            held(2, KB * CELLS, chans, kind=F32),
            held(chans, HID),
            held(HID, chans),
            pltpu.SemaphoreType.DMA((7,)),
            pltpu.SemaphoreType.DMA((21,)),
            pltpu.SemaphoreType.DMA((17,)),
            pltpu.SemaphoreType.REGULAR((3,)),
        ],
        compiler_params=pltpu.CompilerParams(
            collective_id=0, has_side_effects=True, vmem_limit_bytes=24 << 20
        ),
    )(*sources)
    result, field_grad = pl.pallas_call(
        functools.partial(backward_kernel, width),
        name="transposed_mix",
        out_shape=(pltpu.HBM(tiles, BF16), pltpu.HBM(tiles, BF16)),
        in_specs=[vmem] * 6,
        out_specs=(hbm, hbm),
        scratch_shapes=[
            held(*roomy, kind=F32),
            held(*tiles),
            pltpu.SemaphoreType.DMA((2,)),
        ],
        compiler_params=pltpu.CompilerParams(vmem_limit_bytes=16 << 20),
    )(result, grads, back, held_mix, done, begun)
    return unpacked(result, rows, width, chans), unpacked(field_grad, rows, width, chans)


def solution(mesh):
    return jax.shard_map(
        on_device,
        mesh=mesh,
        in_specs=(
            P("lat", "lon", None),
            P(),
            P(None, "lat", None, None),
            P("lat"),
            P(),
            P(),
            P("lat", "lon", None),
        ),
        out_specs=(P("lat", "lon", None), P("lat", "lon", None)),
        check_vma=False,
    )
```
